32 devices in a mesh: grp: 4 (over z), row: 2 (over x), col: 4 (over y, core).
Axes of the slice: x: 2, y: 2, z: 4, core: 2. Of those that a mesh axis runs over, the one named last changes fastest.
Arguments:
- child_fronts: float32 [4, 4096, 4096], P('grp', 'row', 'col'), as said below
- parent_entries: float32 [16384, 4, 4096], P(('grp', 'row'), None, 'col'), as said below
- child_live: int32 [4], replicated, may hold values from 2 to 32, as said below
- quarters: int32 [4, 32], replicated, may hold values from 0 to 3, as said below
Outputs:
- parent_front: float32 [16384, 4, 4096], P(('grp', 'row'), None, 'col')
The draws below stay inside these ranges and needn't reach their ends.
Inputs may be any that keep to these rules, and one draw needn't show every extreme that they name: `child_fronts`: every child front is symmetric and positive definite. `parent_entries`: symmetric and positive definite when read as a matrix of order 16384. `child_live`: one child has all 32 blocks in its structure in every draw. `quarters`: each child's blocks form aligned groups of 16 in a row (blocks 0 to 15, and so on); within one group no quarter is named more than 4 times, and some quarter exactly 4 times.
All inputs are finite; a program needn't handle non-finite values.
Results may differ from the reference program's by a relative error of at most 0.0003.
Values sent between devices are 32-bit elements; how exact they have to be, the bound alone decides.
No kernel may reach another device: no remote copies, remote signals or barrier semaphores. Data moves between devices by JAX's collectives and lax.ppermute only.
A program may use at most 256 MiB of HBM per device.

```python
import math
import jax
import jax.numpy as jnp
from jax import lax

B = 128
CB = 32
KC = 1
KP = 3
NQ = 4
FC = 4096
FP = 16384
RB = 16


def symmetric_block(key, leading_shape, order):
    full_shape = leading_shape + (order, order)
    key_a = jax.random.fold_in(jax.random.fold_in(key, 11), 0)
    key_b = jax.random.fold_in(jax.random.fold_in(key, 11), 1)
    key_d = jax.random.fold_in(jax.random.fold_in(key, 11), 3)
    raw_values = jax.random.truncated_normal(key_a, -6.0, 6.0, full_shape, jnp.float32)
    noise_part = (raw_values + jnp.swapaxes(raw_values, -1, -2)) * (0.25 / math.sqrt(2.0 * order))
    point_coords = jax.random.uniform(key_d, leading_shape + (3, order), jnp.float32)
    squared = jnp.zeros(full_shape, jnp.float32)
    for axis_id in range(3):
        coord_line = point_coords[..., axis_id, :]
        difference = coord_line[..., :, None] - coord_line[..., None, :]
        squared = squared + difference * difference
    kernel = 0.5 * jnp.exp(-jnp.sqrt(squared) / 0.3)
    positions = jnp.arange(order)
    on_diag = positions[:, None] == positions[None, :]
    pivot_values = 1.5 + jax.random.uniform(key_b, leading_shape + (order,), jnp.float32)
    matrix = jnp.where(on_diag, pivot_values[..., :, None], kernel + noise_part)
    return matrix


def draw_child_fronts(key, part):
    return symmetric_block(key, (NQ,), FC)


def draw_parent_entries(key, part):
    return symmetric_block(jax.random.fold_in(key, 5), (), FP).reshape(FP, NQ, FC)


def draw_child_live(key, part):
    key_a, key_b = jax.random.split(jax.random.fold_in(key, 3))
    drawn_live = jax.random.randint(key_a, (NQ,), KC + 1, CB + 1)
    chosen = jax.random.randint(key_b, (), 0, NQ)
    return jnp.where(jnp.arange(NQ) == chosen, CB, drawn_live).astype(jnp.int32)


def draw_quarters(key, part):
    group_count = NQ * (CB // RB)
    key_list = jax.random.split(jax.random.fold_in(key, 7), group_count)
    span_size = max(RB, NQ)
    base_values = (jnp.arange(span_size, dtype=jnp.int32) % NQ).astype(jnp.int32)

    def permute_one(one_key):
        return jax.random.permutation(one_key, base_values)
    shuffled = jax.vmap(permute_one)(key_list)
    return shuffled[:, :RB].reshape(NQ, CB).astype(jnp.int32)


def setup_inputs(seed: int = 0) -> dict:
    arg_keys = jax.random.split(jax.random.key(seed), 5)
    return {
        "child_fronts": draw_child_fronts(jax.random.fold_in(arg_keys[4], 71), 0),
        "parent_entries": draw_parent_entries(jax.random.fold_in(arg_keys[4], 71), 0),
        "child_live": draw_child_live(jax.random.fold_in(arg_keys[4], 71), 0),
        "quarters": draw_quarters(jax.random.fold_in(arg_keys[4], 71), 0),
    }


def partial_factor(front_matrix, pivot_count):
    head_factor = jnp.linalg.cholesky(front_matrix[:pivot_count, :pivot_count])
    below_part = lax.linalg.triangular_solve(head_factor, front_matrix[pivot_count:, :pivot_count], left_side=False, lower=True, transpose_a=True)
    schur_part = front_matrix[pivot_count:, pivot_count:] - jnp.dot(below_part, below_part.T, precision=lax.Precision.HIGHEST)
    return (head_factor, below_part, schur_part)

def reference(child_fronts, parent_entries, child_live, quarters):
    child_count = child_fronts.shape[0]
    leading = KC * B
    trailing_ids = jnp.arange(FC - leading) + leading
    contributions = []
    for child in range(child_count):
        head_factor, below_part, schur_part = partial_factor(child_fronts[child], leading)
        in_tree = trailing_ids < child_live[child] * B
        schur_part = jnp.where(in_tree[:, None] & in_tree[None, :], schur_part, jnp.zeros((), schur_part.dtype))
        schur_part = jnp.pad(schur_part, ((leading, 0), (leading, 0)))
        placement = jnp.repeat(quarters[child], B)
        contributions.append((schur_part, placement))
    rows_list = []
    for quarter_row in range(child_count):
        pieces = []
        for quarter_col in range(child_count):
            summed = parent_entries[quarter_row * FC:(quarter_row + 1) * FC, quarter_col, :]
            for schur_part, placement in contributions:
                row_mask = (placement == quarter_row).astype(summed.dtype)
                col_mask = (placement == quarter_col).astype(summed.dtype)
                summed = summed + schur_part * row_mask[:, None] * col_mask[None, :]
            pieces.append(summed)
        rows_list.append(jnp.concatenate(pieces, axis=1))
    assembled = jnp.concatenate(rows_list, axis=0)
    pivot_count = KP * B
    head_factor, below_part, schur_part = partial_factor(assembled, pivot_count)
    top_rows = jnp.concatenate([head_factor, jnp.zeros((pivot_count, FP - pivot_count), head_factor.dtype)], axis=1)
    bottom_rows = jnp.concatenate([below_part, schur_part], axis=1)
    return jnp.concatenate([top_rows, bottom_rows], axis=0).reshape(FP, child_count, FC)
```

```python
import functools

import jax
import jax.numpy as jnp
from jax import lax
from jax.experimental import pallas as pl
from jax.experimental.pallas import tpu as pltpu
from jax.sharding import PartitionSpec as P

B = 128
KC = 1
KP = 3
FC = 4096
LEAD = KC * B
PIV = KP * B
HIGHEST = lax.Precision.HIGHEST
VMEM_LIMIT = 60 * 1024 * 1024


def dot_nn(a, b, precision=HIGHEST):
    return lax.dot_general(a, b, (((1,), (0,)), ((), ())), precision=precision, preferred_element_type=jnp.float32)


def dot_nt(a, b, precision=HIGHEST):
    return lax.dot_general(a, b, (((1,), (1,)), ((), ())), precision=precision, preferred_element_type=jnp.float32)


def dot_bf(a, b):
    return lax.dot_general(a, b, (((1,), (0,)), ((), ())), preferred_element_type=jnp.float32)


def split(x):
    hi = x.astype(jnp.bfloat16)
    lo = (x - hi.astype(jnp.float32)).astype(jnp.bfloat16)
    return hi, lo


def vmem():
    return pl.BlockSpec(memory_space=pltpu.VMEM)


def smem():
    return pl.BlockSpec(memory_space=pltpu.SMEM)


def invert_factor(block, aug):
    n = block.shape[0]
    rows = lax.broadcasted_iota(jnp.int32, (n, n), 0)
    cols = lax.broadcasted_iota(jnp.int32, (n, n), 1)
    row_ids = lax.broadcasted_iota(jnp.int32, (n, 1), 0)
    lane_ids = lax.broadcasted_iota(jnp.int32, (1, n), 1)
    aug[:, :n] = block
    aug[:, n:] = jnp.where(rows == cols, 1.0, 0.0).astype(jnp.float32)

    def step(k, pivots):
        pivot_row = aug[pl.ds(k, 1), :]
        pivot = jnp.sum(jnp.where(lane_ids == k, pivot_row[:, :n], 0.0), axis=1, keepdims=True)
        body = aug[...]
        column = jnp.sum(jnp.where(cols == k, body[:, :n], 0.0), axis=1, keepdims=True)
        factor = jnp.where(row_ids > k, column / pivot, 0.0)
        aug[...] = body - factor * pivot_row
        return jnp.where(row_ids == k, pivot, pivots)

    pivots = lax.fori_loop(0, n, step, jnp.ones((n, 1), jnp.float32))
    return aug[:, n:] / jnp.sqrt(pivots)


def child_kernel(pos, live, quarters, block, strip, prow, lead_rows, brow3, bcol3, panel, aug, brow):
    rows_here, cols_here = strip.shape[0], prow.shape[1]
    grp, row, col = pos[0], pos[1], pos[2]
    live_end = live[grp] * B
    inverse = invert_factor(block[...], aug)
    row_ids = row * rows_here + lax.broadcasted_iota(jnp.int32, (rows_here, 1), 0)
    col_ids = col * cols_here + lax.broadcasted_iota(jnp.int32, (1, cols_here), 1)
    live_rows = (row_ids >= LEAD) & (row_ids < live_end)
    live_cols = (col_ids >= LEAD) & (col_ids < live_end)
    brow[...] = jnp.where(live_rows, dot_nt(strip[...], inverse), 0.0)
    bcol = jnp.where(live_cols, dot_nn(inverse, prow[...]), 0.0)
    hi, lo = split(brow[...])
    brow3[:, :LEAD] = hi
    brow3[:, LEAD : 2 * LEAD] = hi
    brow3[:, 2 * LEAD :] = lo
    hi, lo = split(bcol)
    bcol3[:LEAD] = hi
    bcol3[LEAD : 2 * LEAD] = lo
    bcol3[2 * LEAD :] = hi
    for k in range(KC, KP):
        at = (k - KC) * B
        keep = live_cols & (k * B < live_end) & (quarters[grp, k] == 0)
        update = dot_nn(brow[k * B : (k + 1) * B, :], bcol)
        panel[at : at + B, :] = jnp.where(keep, lead_rows[at : at + B, :] - update, 0.0)


def outgoing_kernel(pos, live, quarters, front, brow3, bcol3, out, gathered, picked):
    rows_here, cols_here = front.shape
    row_blocks = rows_here // B
    slots = out.shape[1] // B
    grp, row, col = pos[0], pos[1], pos[2]
    live_end = live[grp] * B
    target = pl.program_id(0)

    def pick(b, count):
        hit = quarters[grp, row * row_blocks + b] == target

        @pl.when(hit & (count < slots))
        def _():
            picked[count] = b

        return count + hit.astype(jnp.int32)

    lax.fori_loop(0, row_blocks, pick, jnp.int32(0))
    for s in range(slots):
        at = pl.multiple_of(picked[s] * B, B)
        gathered[s * B : (s + 1) * B, :] = brow3[pl.ds(at, B), :]
    width = min(256, cols_here)
    for n in range(cols_here // width):
        cut = slice(n * width, (n + 1) * width)
        product = dot_bf(gathered[...], bcol3[:, cut])
        col_ids = col * cols_here + n * width + lax.broadcasted_iota(jnp.int32, (1, width), 1)
        live_cols = (col_ids >= LEAD) & (col_ids < live_end)
        for s in range(slots):
            at = pl.multiple_of(picked[s] * B, B)
            first = row * rows_here + at
            keep = live_cols & (first >= LEAD) & (first < live_end)
            value = front[pl.ds(at, B), cut] - product[s * B : (s + 1) * B]
            out[0, s * B : (s + 1) * B, cut] = jnp.where(keep, value, 0.0)


def head_kernel(head, inverse, work, factor, aug):
    work[...] = head[...]
    inverse[...] = jnp.zeros_like(inverse)
    for k in range(KP):
        kk = slice(k * B, (k + 1) * B)
        diag = invert_factor(work[kk, kk], aug)
        inverse[kk, kk] = diag
        for i in range(k + 1, KP):
            ii = slice(i * B, (i + 1) * B)
            factor[ii, kk] = dot_nt(work[ii, kk], diag)
        for i in range(k + 1, KP):
            for j in range(k + 1, i + 1):
                ii, jj = slice(i * B, (i + 1) * B), slice(j * B, (j + 1) * B)
                work[ii, jj] = work[ii, jj] - dot_nt(factor[ii, kk], factor[jj, kk])
        for j in range(k):
            jj = slice(j * B, (j + 1) * B)
            total = jnp.zeros((B, B), jnp.float32)
            for i in range(j, k):
                ii = slice(i * B, (i + 1) * B)
                total = total + dot_nn(factor[kk, ii], inverse[ii, jj])
            inverse[kk, jj] = -dot_nn(diag, total)


def columns_kernel(pos, quarters, inverse, entries, panels, lc3, mine, placed):
    groups, _, cols_here = panels.shape
    col_blocks = cols_here // B
    grp, col = pos[0], pos[2]
    quarter = pl.program_id(0)
    placed[...] = jnp.zeros_like(placed)
    for g in range(groups):
        for b in range(col_blocks):
            cut = slice(b * B, (b + 1) * B)

            @pl.when(quarters[g, col * col_blocks + b] == quarter)
            def _(g=g, cut=cut):
                placed[:, cut] += panels[g, :, cut]

    value = dot_nt(inverse[...], entries[...]) + dot_nn(inverse[:, LEAD:], placed[...])
    hi, lo = split(value)
    lc3[:PIV] = hi
    lc3[PIV : 2 * PIV] = lo
    lc3[2 * PIV :] = hi

    @pl.when(quarter == grp)
    def _():
        mine[...] = value


def rows_kernel(pos, across, lr, lr3):
    height = lr.shape[0]
    value = jnp.transpose(across[...])
    first = pos[3] + pl.program_id(0) * height
    row_ids = first + lax.broadcasted_iota(jnp.int32, (height, PIV), 0)
    inside = lax.broadcasted_iota(jnp.int32, (height, PIV), 1)
    value = jnp.where(inside <= row_ids, value, 0.0)
    lr[...] = value
    hi, lo = split(value)
    lr3[:, :PIV] = hi
    lr3[:, PIV : 2 * PIV] = hi
    lr3[:, 2 * PIV :] = lo


def final_kernel(pos, quarters, arrived, lr, lr3, lc3, entries, out, acc, slot_of):
    groups, _, cols_here = arrived.shape
    height = entries.shape[0]
    pair = entries.shape[1] // groups
    width = pair * B
    row_blocks = slot_of.shape[1]
    blocks = height // B
    grp, row, col, first_row = pos[0], pos[1], pos[2], pos[3]
    rb, p = pl.program_id(0), pl.program_id(1)

    @pl.when((rb == 0) & (p == 0))
    def _():
        for g in range(groups):

            def note(b, count, g=g):
                hit = quarters[g, row * row_blocks + b] == grp
                slot_of[g, b] = jnp.where(hit, count, -1)
                return count + hit.astype(jnp.int32)

            lax.fori_loop(0, row_blocks, note, jnp.int32(0))

    start = pl.multiple_of(p * width, width)
    left = lr3[...]
    for u in range(groups):
        product = dot_bf(left, lc3[:, pl.ds(pl.multiple_of(u * cols_here + start, width), width)])
        for h in range(pair):
            acc[h * groups + u] = -product[:, h * B : (h + 1) * B]

    for g in range(groups):
        for b in range(blocks):
            slot = slot_of[g, rb * blocks + b]

            @pl.when(slot >= 0)
            def _(g=g, b=b, slot=slot):
                at = pl.multiple_of(slot * B, B)
                for h in range(pair):
                    place = quarters[g, col * (cols_here // B) + p * pair + h]
                    value = arrived[g, pl.ds(at, B), pl.ds(pl.multiple_of(start + h * B, B), B)]
                    acc[h * groups + place, b * B : (b + 1) * B, :] += value

    step = 32
    first = first_row + rb * height

    def plain(i, carry):
        at = pl.multiple_of(i * step, step)
        value = jnp.swapaxes(acc[:, pl.ds(at, step), :], 0, 1)
        out[pl.ds(at, step)] = entries[pl.ds(at, step)] + value
        return carry

    begin_col = col * cols_here + start
    special = (first < PIV) | (begin_col < PIV)

    @pl.when(jnp.logical_not(special))
    def _():
        lax.fori_loop(0, height // step, plain, 0)

    @pl.when(special)
    def _():
        row_ids = first + lax.broadcasted_iota(jnp.int32, (height, 1), 0)
        for h in range(pair):
            for u in range(groups):
                here = begin_col + h * B
                is_pivot = (here < PIV) if u == 0 else False
                if u == 0:
                    strip = lr[:, pl.ds(pl.multiple_of(jnp.where(is_pivot, here, 0), B), B)]
                    other = jnp.where(row_ids < PIV, 0.0, acc[h * groups])
                    acc[h * groups] = jnp.where(is_pivot, strip, other)
                else:
                    acc[h * groups + u] = jnp.where(row_ids < PIV, 0.0, acc[h * groups + u])

        def masked(i, carry):
            at = pl.multiple_of(i * step, step)
            value = jnp.swapaxes(acc[:, pl.ds(at, step), :], 0, 1)
            shape = (step, pair * groups, B)
            ids = first + at + lax.broadcasted_iota(jnp.int32, shape, 0)
            which = lax.broadcasted_iota(jnp.int32, shape, 1)
            pivot_col = (which % groups == 0) & (begin_col + (which // groups) * B < PIV)
            keep = (ids >= PIV) & jnp.logical_not(pivot_col)
            out[pl.ds(at, step)] = jnp.where(keep, entries[pl.ds(at, step)], 0.0) + value
            return carry

        lax.fori_loop(0, height // step, masked, 0)


def params(**kw):
    return pltpu.CompilerParams(vmem_limit_bytes=VMEM_LIMIT, **kw)


def bcast(value, axis, size):
    here = lax.axis_index(axis)
    stride = size // 2
    while stride >= 1:
        pairs = [(i, i + stride) for i in range(0, size, 2 * stride)]
        moved = lax.ppermute(value, axis, pairs)
        value = jnp.where(here % (2 * stride) == stride, moved, value)
        stride //= 2
    return value


def shards(child_fronts, parent_entries, child_live, quarters):
    front = child_fronts[0]
    rows_here, cols_here = front.shape
    groups, rows_n, cols_n = (lax.axis_size(a) for a in ("grp", "row", "col"))
    grp, row, col = (lax.axis_index(a) for a in ("grp", "row", "col"))
    row_blocks = rows_here // B
    slots = row_blocks // groups
    spans = rows_here // cols_here
    first_row = (grp * rows_n + row) * rows_here
    ids = jnp.arange(8, dtype=jnp.int32)
    pos = jnp.where(ids == 0, grp, jnp.where(ids == 1, row, jnp.where(ids == 2, col, first_row)))
    pos = pos.astype(jnp.int32)
    f32, bf16 = jnp.float32, jnp.bfloat16
    shape = jax.ShapeDtypeStruct

    own = parent_entries[:, 0, : min(PIV, cols_here)]
    for other in range(1, -(-PIV // cols_here)):
        wide = min(cols_here, PIV - other * cols_here)
        own = jnp.concatenate([own, lax.ppermute(parent_entries[:, 0, :wide], "col", [(other, 0)])], axis=1)
    part = cols_here // rows_n
    piece = jnp.zeros((part, PIV), f32)
    for h in range(spans):
        for r in range(rows_n):
            at = h * cols_here + r * part
            pairs = [(s * cols_n, r * cols_n + s * spans + h) for s in range(rows_n)]
            piece = piece + lax.ppermute(own[at : at + part], ("row", "col"), pairs)
    entries_c = lax.all_gather(piece, ("grp", "row"), tiled=True)

    strip = bcast(front[:, :LEAD], "col", cols_n)
    corner = bcast(front[:LEAD, :LEAD], "col", cols_n)
    payload = bcast(jnp.concatenate([front[:LEAD], corner], axis=1), "row", rows_n)
    brow3, bcol3, panel = pl.pallas_call(
        child_kernel,
        out_shape=(
            shape((rows_here, 3 * LEAD), bf16),
            shape((3 * LEAD, cols_here), bf16),
            shape((PIV - LEAD, cols_here), f32),
        ),
        in_specs=[smem(), smem(), smem(), vmem(), vmem(), vmem(), vmem()],
        out_specs=(vmem(), vmem(), vmem()),
        scratch_shapes=[pltpu.VMEM((LEAD, 2 * LEAD), f32), pltpu.VMEM((rows_here, LEAD), f32)],
        compiler_params=params(),
        name="child",
    )(pos, child_live, quarters, payload[:, cols_here:], strip, payload[:, :cols_here], front[LEAD:PIV])

    head = jnp.zeros((PIV, PIV), f32)
    for other in range(-(-PIV // cols_here)):
        wide = min(cols_here, PIV - other * cols_here)
        mine = (row == 0) & (col == other)
        at = other * cols_here
        which = lax.dynamic_slice_in_dim(quarters, grp, 1, 0)[0, at // B : (at + wide) // B]
        keep = mine & (jnp.repeat(which, B) == 0)
        first = jnp.where(mine & (grp == 0), parent_entries[:PIV, 0, :wide], 0.0)
        added = jnp.where(keep[None, :], panel[:, :wide], 0.0)
        head = head.at[:, at : at + wide].add(first + jnp.pad(added, ((LEAD, 0), (0, 0))))
    head = lax.psum(head, ("grp", "row", "col"))

    share = (PIV - LEAD) // rows_n
    panel_piece = jnp.where(row == 0, panel[:share], 0.0)
    for r in range(1, rows_n):
        panel_piece = panel_piece + lax.ppermute(panel[r * share : (r + 1) * share], "row", [(0, r)])
    panels = lax.all_gather(panel_piece, ("grp", "row"), tiled=True).reshape(groups, PIV - LEAD, cols_here)

    outgoing = pl.pallas_call(
        outgoing_kernel,
        grid=(groups,),
        out_shape=shape((groups, slots * B, cols_here), f32),
        in_specs=[smem(), smem(), smem(), vmem(), vmem(), vmem()],
        out_specs=pl.BlockSpec((1, slots * B, cols_here), lambda d: (d, 0, 0)),
        scratch_shapes=[pltpu.VMEM((slots * B, 3 * LEAD), bf16), pltpu.SMEM((slots,), jnp.int32)],
        compiler_params=params(),
        name="outgoing",
    )(pos, child_live, quarters, front, brow3, bcol3)
    arrived = lax.all_to_all(outgoing, "grp", split_axis=0, concat_axis=0, tiled=True)

    inverse = pl.pallas_call(
        head_kernel,
        out_shape=shape((PIV, PIV), f32),
        in_specs=[vmem()],
        out_specs=vmem(),
        scratch_shapes=[pltpu.VMEM((PIV, PIV), f32), pltpu.VMEM((PIV, PIV), f32), pltpu.VMEM((B, 2 * B), f32)],
        compiler_params=params(),
        cost_estimate=pl.CostEstimate(flops=10**9, bytes_accessed=10**8, transcendentals=0),
        name="head",
    )(head)

    lc3, mine = pl.pallas_call(
        columns_kernel,
        grid=(groups,),
        out_shape=(shape((3 * PIV, groups * cols_here), bf16), shape((PIV, cols_here), f32)),
        in_specs=[
            smem(),
            smem(),
            vmem(),
            pl.BlockSpec((cols_here, PIV), lambda u: (u, 0)),
            vmem(),
        ],
        out_specs=(pl.BlockSpec((3 * PIV, cols_here), lambda u: (0, u)), vmem()),
        scratch_shapes=[pltpu.VMEM((PIV - LEAD, cols_here), f32)],
        compiler_params=params(),
        cost_estimate=pl.CostEstimate(flops=10**10, bytes_accessed=3 * 10**7, transcendentals=0),
        name="columns",
    )(pos, quarters, inverse, entries_c, panels)

    y_n = cols_n // spans
    y_here = (col // spans - row) % y_n
    stride = y_n // 2
    while stride >= 1:
        pairs = []
        for r in range(rows_n):
            for y in range(0, y_n, 2 * stride):
                for k in range(spans):
                    source, target = (r + y) % y_n * spans + k, (r + y + stride) % y_n * spans + k
                    pairs.append((r * cols_n + source, r * cols_n + target))
        moved = lax.ppermute(mine, ("row", "col"), pairs)
        mine = jnp.where(y_here % (2 * stride) == stride, moved, mine)
        stride //= 2
    parts = [mine]
    for k in range(1, spans):
        pairs = [(y * spans + i, y * spans + (i + k) % spans) for y in range(y_n) for i in range(spans)]
        parts.append(lax.ppermute(mine, "col", pairs))
    inner = col % spans
    across = jnp.concatenate(
        [
            functools.reduce(lambda a, k: jnp.where((inner - s) % spans == k, parts[k], a), range(1, spans), parts[0])
            for s in range(spans)
        ],
        axis=1,
    )
    tall = min(256, rows_here)
    lr, lr3 = pl.pallas_call(
        rows_kernel,
        grid=(rows_here // tall,),
        out_shape=(shape((rows_here, PIV), f32), shape((rows_here, 3 * PIV), bf16)),
        in_specs=[smem(), pl.BlockSpec((PIV, tall), lambda i: (0, i))],
        out_specs=(pl.BlockSpec((tall, PIV), lambda i: (i, 0)), pl.BlockSpec((tall, 3 * PIV), lambda i: (i, 0))),
        compiler_params=params(),
        name="rows",
    )(pos, across)

    lanes = cols_here // B
    pair = 2
    tall = min(512, rows_here)
    view = parent_entries.reshape(rows_here, groups, lanes, B).transpose(0, 2, 1, 3).reshape(rows_here, lanes * groups, B)
    result = pl.pallas_call(
        final_kernel,
        grid=(rows_here // tall, lanes // pair),
        out_shape=shape((rows_here, lanes * groups, B), f32),
        in_specs=[
            smem(),
            smem(),
            vmem(),
            pl.BlockSpec((tall, PIV), lambda i, p: (i, 0)),
            pl.BlockSpec((tall, 3 * PIV), lambda i, p: (i, 0)),
            vmem(),
            pl.BlockSpec((tall, pair * groups, B), lambda i, p: (i, p, 0)),
        ],
        out_specs=pl.BlockSpec((tall, pair * groups, B), lambda i, p: (i, p, 0)),
        scratch_shapes=[pltpu.VMEM((pair * groups, tall, B), f32), pltpu.SMEM((groups, row_blocks), jnp.int32)],
        compiler_params=params(),
        name="final",
    )(pos, quarters, arrived, lr, lr3, lc3, view)
    return result.reshape(rows_here, lanes, groups, B).transpose(0, 2, 1, 3).reshape(rows_here, groups, cols_here)


def solution(mesh):
    in_specs = (P("grp", "row", "col"), P(("grp", "row"), None, "col"), P(), P())
    out_specs = P(("grp", "row"), None, "col")
    return jax.shard_map(shards, mesh=mesh, in_specs=in_specs, out_specs=out_specs, check_vma=False)
```

```python
import functools

import jax
import jax.numpy as jnp
from jax import lax
from jax.experimental import pallas as pl
from jax.experimental.pallas import tpu as pltpu
from jax.sharding import PartitionSpec as P

B = 128
KC = 1
KP = 3
FC = 4096
LEAD = KC * B
PIV = KP * B
HIGHEST = lax.Precision.HIGHEST
VMEM_LIMIT = 60 * 1024 * 1024


def dot_nn(a, b, precision=HIGHEST):
    return lax.dot_general(a, b, (((1,), (0,)), ((), ())), precision=precision, preferred_element_type=jnp.float32)


def dot_nt(a, b, precision=HIGHEST):
    return lax.dot_general(a, b, (((1,), (1,)), ((), ())), precision=precision, preferred_element_type=jnp.float32)


def dot_bf(a, b):
    return lax.dot_general(a, b, (((1,), (0,)), ((), ())), preferred_element_type=jnp.float32)


def split(x):
    hi = x.astype(jnp.bfloat16)
    lo = (x - hi.astype(jnp.float32)).astype(jnp.bfloat16)
    return hi, lo


def vmem():
    return pl.BlockSpec(memory_space=pltpu.VMEM)


def smem():
    return pl.BlockSpec(memory_space=pltpu.SMEM)


def invert_factor(block, aug):
    n = block.shape[0]
    rows = lax.broadcasted_iota(jnp.int32, (n, n), 0)
    cols = lax.broadcasted_iota(jnp.int32, (n, n), 1)
    row_ids = lax.broadcasted_iota(jnp.int32, (n, 1), 0)
    lane_ids = lax.broadcasted_iota(jnp.int32, (1, n), 1)
    aug[:, :n] = block
    aug[:, n:] = jnp.where(rows == cols, 1.0, 0.0).astype(jnp.float32)

    many = 4

    def step(i, pivots):
        k = i * many
        rows_k = [aug[pl.ds(k + j, 1), :] for j in range(many)]
        body = aug[...]
        columns = [jnp.sum(jnp.where(cols == k + j, body[:, :n], 0.0), axis=1, keepdims=True) for j in range(many)]
        small = [
            [jnp.sum(jnp.where(lane_ids == k + b, rows_k[a][:, :n], 0.0), axis=1, keepdims=True) for b in range(many)]
            for a in range(many)
        ]
        factors = []
        for a in range(many):
            scale = 1.0 / small[a][a]
            for b in range(a + 1, many):
                ratio = small[a][b] * scale
                rows_k[b] = rows_k[b] - ratio * rows_k[a]
                columns[b] = columns[b] - columns[a] * ratio
                for c in range(b, many):
                    small[b][c] = small[b][c] - ratio * small[a][c]
            factors.append(jnp.where(row_ids >= k + many, columns[a] * scale, 0.0))
            pivots = jnp.where(row_ids == k + a, small[a][a], pivots)
        for a in range(many):
            body = body - factors[a] * rows_k[a]
        aug[...] = body
        for a in range(1, many):
            aug[pl.ds(k + a, 1), :] = rows_k[a]
        return pivots

    pivots = lax.fori_loop(0, n // many, step, jnp.ones((n, 1), jnp.float32))
    return aug[:, n:] / jnp.sqrt(pivots)


def extract_kernel(groups, view, out):
    for h in range(out.shape[1] // B):
        out[:, h * B : (h + 1) * B] = view[:, h * groups, :]


def child_kernel(pos, live, quarters, block, strip, prow, lead_rows, brow3, bcol3, panel, aug, brow):
    rows_here, cols_here = strip.shape[0], prow.shape[1]
    grp, row, col = pos[0], pos[1], pos[2]
    live_end = live[grp] * B
    inverse = invert_factor(block[...], aug)
    row_ids = row * rows_here + lax.broadcasted_iota(jnp.int32, (rows_here, 1), 0)
    col_ids = col * cols_here + lax.broadcasted_iota(jnp.int32, (1, cols_here), 1)
    live_rows = (row_ids >= LEAD) & (row_ids < live_end)
    live_cols = (col_ids >= LEAD) & (col_ids < live_end)
    brow[...] = jnp.where(live_rows, dot_nt(strip[...], inverse), 0.0)
    bcol = jnp.where(live_cols, dot_nn(inverse, prow[...]), 0.0)
    hi, lo = split(brow[...])
    brow3[:, :LEAD] = hi
    brow3[:, LEAD : 2 * LEAD] = hi
    brow3[:, 2 * LEAD :] = lo
    hi, lo = split(bcol)
    bcol3[:LEAD] = hi
    bcol3[LEAD : 2 * LEAD] = lo
    bcol3[2 * LEAD :] = hi
    for k in range(KC, KP):
        at = (k - KC) * B
        keep = live_cols & (k * B < live_end) & (quarters[grp, k] == 0)
        update = dot_nn(brow[k * B : (k + 1) * B, :], bcol)
        panel[at : at + B, :] = jnp.where(keep, lead_rows[at : at + B, :] - update, 0.0)


def outgoing_kernel(pos, live, quarters, front, brow3, bcol3, out, gathered, picked):
    rows_here, cols_here = front.shape
    row_blocks = rows_here // B
    slots = out.shape[1] // B
    grp, row, col = pos[0], pos[1], pos[2]
    live_end = live[grp] * B
    target = pl.program_id(0)

    def pick(b, count):
        hit = quarters[grp, row * row_blocks + b] == target

        @pl.when(hit & (count < slots))
        def _():
            picked[count] = b

        return count + hit.astype(jnp.int32)

    lax.fori_loop(0, row_blocks, pick, jnp.int32(0))
    for s in range(slots):
        at = pl.multiple_of(picked[s] * B, B)
        gathered[s * B : (s + 1) * B, :] = brow3[pl.ds(at, B), :]
    width = min(256, cols_here)
    for n in range(cols_here // width):
        cut = slice(n * width, (n + 1) * width)
        product = dot_bf(gathered[...], bcol3[:, cut])
        col_ids = col * cols_here + n * width + lax.broadcasted_iota(jnp.int32, (1, width), 1)
        live_cols = (col_ids >= LEAD) & (col_ids < live_end)
        for s in range(slots):
            at = pl.multiple_of(picked[s] * B, B)
            first = row * rows_here + at
            keep = live_cols & (first >= LEAD) & (first < live_end)
            value = front[pl.ds(at, B), cut] - product[s * B : (s + 1) * B]
            out[0, s * B : (s + 1) * B, cut] = jnp.where(keep, value, 0.0)


def head_kernel(head, inverse, work, factor, aug):
    work[...] = head[...]
    inverse[...] = jnp.zeros_like(inverse)
    for k in range(KP):
        kk = slice(k * B, (k + 1) * B)
        diag = invert_factor(work[kk, kk], aug)
        inverse[kk, kk] = diag
        for i in range(k + 1, KP):
            ii = slice(i * B, (i + 1) * B)
            factor[ii, kk] = dot_nt(work[ii, kk], diag)
        for i in range(k + 1, KP):
            for j in range(k + 1, i + 1):
                ii, jj = slice(i * B, (i + 1) * B), slice(j * B, (j + 1) * B)
                work[ii, jj] = work[ii, jj] - dot_nt(factor[ii, kk], factor[jj, kk])
        for j in range(k):
            jj = slice(j * B, (j + 1) * B)
            total = jnp.zeros((B, B), jnp.float32)
            for i in range(j, k):
                ii = slice(i * B, (i + 1) * B)
                total = total + dot_nn(factor[kk, ii], inverse[ii, jj])
            inverse[kk, jj] = -dot_nn(diag, total)


def place_pieces(pos, quarters, pieces, panels, quarter, entries, placed):
    groups = quarters.shape[0]
    rows_n = len(pieces) // groups
    part, share = pieces[0].shape[0], panels[0].shape[0]
    col_blocks = placed.shape[1] // B
    grp, row, col = pos[0], pos[1], pos[2]
    placed[...] = jnp.zeros_like(placed)
    for s in range(groups):
        source = lax.rem(grp + groups - s, groups)

        @pl.when(source == quarter)
        def _(s=s):
            for t in range(rows_n):
                at = pl.multiple_of(lax.rem(row + rows_n - t, rows_n) * part, part)
                entries[pl.ds(at, part), :] = pieces[s * rows_n + t][...]

        for b in range(col_blocks):
            cut = slice(b * B, (b + 1) * B)

            @pl.when(quarters[source, col * col_blocks + b] == quarter)
            def _(s=s, cut=cut):
                for t in range(rows_n):
                    at = pl.multiple_of(lax.rem(row + rows_n - t, rows_n) * share, share)
                    placed[pl.ds(at, share), cut] += panels[s * rows_n + t][:, cut]


def columns_kernel(pos, quarters, inverse, *refs):
    lc3, entries, placed = refs[-3:]
    count = (len(refs) - 3) // 2
    place_pieces(pos, quarters, refs[:count], refs[count : 2 * count], pl.program_id(0), entries, placed)
    value = dot_nt(inverse[...], entries[...]) + dot_nn(inverse[:, LEAD:], placed[...])
    hi, lo = split(value)
    lc3[:PIV] = hi
    lc3[PIV : 2 * PIV] = lo
    lc3[2 * PIV :] = hi


def mine_kernel(pos, quarters, *refs):
    mine, entries, placed = refs[-3:]
    count = (len(refs) - 3) // 2
    place_pieces(pos, quarters, refs[:count], refs[count : 2 * count], pos[0], entries, placed)
    for k in range(KP):
        kk = slice(k * B, (k + 1) * B)
        value = jnp.transpose(entries[:, kk])
        mine[kk] = value if k < KC else value + placed[(k - KC) * B : (k - KC + 1) * B]


def rows_kernel(pos, inverse, across, lr, lr3):
    height = lr.shape[0]
    value = jnp.transpose(dot_nn(inverse[...], across[...]))
    first = pos[3] + pl.program_id(0) * height
    row_ids = first + lax.broadcasted_iota(jnp.int32, (height, PIV), 0)
    inside = lax.broadcasted_iota(jnp.int32, (height, PIV), 1)
    value = jnp.where(inside <= row_ids, value, 0.0)
    lr[...] = value
    hi, lo = split(value)
    lr3[:, :PIV] = hi
    lr3[:, PIV : 2 * PIV] = hi
    lr3[:, 2 * PIV :] = lo


def final_kernel(pos, quarters, arrived, lr, lr3, lc3, entries, out, acc, slot_of):
    groups, _, cols_here = arrived.shape
    height = entries.shape[0]
    pair = entries.shape[1] // groups
    width = pair * B
    row_blocks = slot_of.shape[1]
    blocks = height // B
    grp, row, col, first_row = pos[0], pos[1], pos[2], pos[3]
    rb, p = pl.program_id(0), pl.program_id(1)

    @pl.when((rb == 0) & (p == 0))
    def _():
        for g in range(groups):

            def note(b, count, g=g):
                hit = quarters[g, row * row_blocks + b] == grp
                slot_of[g, b] = jnp.where(hit, count, -1)
                return count + hit.astype(jnp.int32)

            lax.fori_loop(0, row_blocks, note, jnp.int32(0))

    start = pl.multiple_of(p * width, width)
    left = lr3[...]
    for u in range(groups):
        product = dot_bf(left, lc3[:, pl.ds(pl.multiple_of(u * cols_here + start, width), width)])
        for h in range(pair):
            acc[h * groups + u] = -product[:, h * B : (h + 1) * B]

    for g in range(groups):
        for b in range(blocks):
            slot = slot_of[g, rb * blocks + b]

            @pl.when(slot >= 0)
            def _(g=g, b=b, slot=slot):
                at = pl.multiple_of(slot * B, B)
                for h in range(pair):
                    place = quarters[g, col * (cols_here // B) + p * pair + h]
                    value = arrived[g, pl.ds(at, B), pl.ds(pl.multiple_of(start + h * B, B), B)]
                    acc[h * groups + place, b * B : (b + 1) * B, :] += value

    step = 32
    first = first_row + rb * height

    def plain(i, carry):
        at = pl.multiple_of(i * step, step)
        value = jnp.swapaxes(acc[:, pl.ds(at, step), :], 0, 1)
        out[pl.ds(at, step)] = entries[pl.ds(at, step)] + value
        return carry

    begin_col = col * cols_here + start
    special = (first < PIV) | (begin_col < PIV)

    @pl.when(jnp.logical_not(special))
    def _():
        lax.fori_loop(0, height // step, plain, 0)

    @pl.when(special)
    def _():
        row_ids = first + lax.broadcasted_iota(jnp.int32, (height, 1), 0)
        for h in range(pair):
            for u in range(groups):
                here = begin_col + h * B
                is_pivot = (here < PIV) if u == 0 else False
                if u == 0:
                    strip = lr[:, pl.ds(pl.multiple_of(jnp.where(is_pivot, here, 0), B), B)]
                    other = jnp.where(row_ids < PIV, 0.0, acc[h * groups])
                    acc[h * groups] = jnp.where(is_pivot, strip, other)
                else:
                    acc[h * groups + u] = jnp.where(row_ids < PIV, 0.0, acc[h * groups + u])

        def masked(i, carry):
            at = pl.multiple_of(i * step, step)
            value = jnp.swapaxes(acc[:, pl.ds(at, step), :], 0, 1)
            shape = (step, pair * groups, B)
            ids = first + at + lax.broadcasted_iota(jnp.int32, shape, 0)
            which = lax.broadcasted_iota(jnp.int32, shape, 1)
            pivot_col = (which % groups == 0) & (begin_col + (which // groups) * B < PIV)
            keep = (ids >= PIV) & jnp.logical_not(pivot_col)
            out[pl.ds(at, step)] = jnp.where(keep, entries[pl.ds(at, step)], 0.0) + value
            return carry

        lax.fori_loop(0, height // step, masked, 0)


def params(**kw):
    return pltpu.CompilerParams(vmem_limit_bytes=VMEM_LIMIT, **kw)


def cost(us):
    return pl.CostEstimate(flops=10**6, bytes_accessed=us * 3_500_000, transcendentals=0)


def bcast(value, axis, size):
    here = lax.axis_index(axis)
    stride = size // 2
    while stride >= 1:
        pairs = [(i, i + stride) for i in range(0, size, 2 * stride)]
        moved = lax.ppermute(value, axis, pairs)
        value = jnp.where(here % (2 * stride) == stride, moved, value)
        stride //= 2
    return value


def ring_shift(value, axis, size, by):
    return lax.ppermute(value, axis, [(i, (i + by) % size) for i in range(size)])


def step_up(value, groups):
    return lax.ppermute(value, "grp", [(i, i + 1) for i in range(groups - 1)])


def step_down(value, groups):
    return lax.ppermute(value, "grp", [(i + 1, i) for i in range(groups - 1)])


def across_rows(planes, rows_n):
    return [v if t == 0 else ring_shift(v, "row", rows_n, t) for v in planes for t in range(rows_n)]


def shards(child_fronts, parent_entries, child_live, quarters):
    front = child_fronts[0]
    rows_here, cols_here = front.shape
    groups, rows_n, cols_n = (lax.axis_size(a) for a in ("grp", "row", "col"))
    grp, row, col = (lax.axis_index(a) for a in ("grp", "row", "col"))
    row_blocks = rows_here // B
    slots = row_blocks // groups
    spans = rows_here // cols_here
    first_row = (grp * rows_n + row) * rows_here
    ids = jnp.arange(8, dtype=jnp.int32)
    pos = jnp.where(ids == 0, grp, jnp.where(ids == 1, row, jnp.where(ids == 2, col, first_row)))
    pos = pos.astype(jnp.int32)
    f32, bf16 = jnp.float32, jnp.bfloat16
    shape = jax.ShapeDtypeStruct

    lanes = cols_here // B
    view = parent_entries.reshape(rows_here, groups, lanes, B).transpose(0, 2, 1, 3).reshape(rows_here, lanes * groups, B)
    wide = min(PIV, cols_here)
    tall = min(512, rows_here)
    deep = -(-wide // B * groups // 8) * 8
    own = pl.pallas_call(
        functools.partial(extract_kernel, groups),
        grid=(rows_here // tall,),
        out_shape=shape((rows_here, wide), f32),
        in_specs=[pl.BlockSpec((tall, deep, B), lambda i: (i, 0, 0))],
        out_specs=pl.BlockSpec((tall, wide), lambda i: (i, 0)),
        compiler_params=params(),
        cost_estimate=cost(6),
        name="extract",
    )(view)
    first_own = own
    for other in range(1, -(-PIV // cols_here)):
        wide = min(cols_here, PIV - other * cols_here)
        own = jnp.concatenate([own, lax.ppermute(first_own[:, :wide], "col", [(other, 0)])], axis=1)
    part = cols_here // rows_n
    pieces = []
    for h in range(spans):
        for r in range(rows_n):
            at = (h * rows_n + r) * part
            pairs = [(s * cols_n, r * cols_n + s * spans + h) for s in range(rows_n)]
            pieces.append(lax.ppermute(own[at : at + part], ("row", "col"), pairs))
    piece = functools.reduce(lambda a, b: a + b, pieces)
    up = [piece, step_up(piece, groups)] + [None] * (groups - 2)
    down = [piece, step_down(piece, groups)] + [None] * (groups - 2)

    strip = bcast(front[:, :LEAD], "col", cols_n)
    corner = bcast(front[:LEAD, :LEAD], "col", cols_n)
    payload = bcast(jnp.concatenate([front[:LEAD], corner], axis=1), "row", rows_n)
    strip, payload, up[1], down[1] = lax.optimization_barrier((strip, payload, up[1], down[1]))
    for k in range(2, groups):
        up[k], down[k] = step_up(up[k - 1], groups), step_down(down[k - 1], groups)
    brow3, bcol3, panel = pl.pallas_call(
        child_kernel,
        out_shape=(
            shape((rows_here, 3 * LEAD), bf16),
            shape((3 * LEAD, cols_here), bf16),
            shape((PIV - LEAD, cols_here), f32),
        ),
        in_specs=[smem(), smem(), smem(), vmem(), vmem(), vmem(), vmem()],
        out_specs=(vmem(), vmem(), vmem()),
        scratch_shapes=[pltpu.VMEM((LEAD, 2 * LEAD), f32), pltpu.VMEM((rows_here, LEAD), f32)],
        compiler_params=params(),
        cost_estimate=cost(20),
        name="child",
    )(pos, child_live, quarters, payload[:, cols_here:], strip, payload[:, :cols_here], front[LEAD:PIV])

    share = (PIV - LEAD) // rows_n
    panel_piece = jnp.where(row == 0, panel[:share], 0.0)
    for r in range(1, rows_n):
        panel_piece = panel_piece + lax.ppermute(panel[r * share : (r + 1) * share], "row", [(0, r)])

    outgoing = pl.pallas_call(
        outgoing_kernel,
        grid=(groups,),
        out_shape=shape((groups, slots * B, cols_here), f32),
        in_specs=[smem(), smem(), smem(), vmem(), vmem(), vmem()],
        out_specs=pl.BlockSpec((1, slots * B, cols_here), lambda d: (d, 0, 0)),
        scratch_shapes=[pltpu.VMEM((slots * B, 3 * LEAD), bf16), pltpu.SMEM((slots,), jnp.int32)],
        compiler_params=params(),
        cost_estimate=cost(10),
        name="outgoing",
    )(pos, child_live, quarters, front, brow3, bcol3)

    planes = [panel_piece] + [ring_shift(panel_piece, "grp", groups, s) for s in range(1, groups)]
    outgoing, up[1:], down[1:], planes[1:] = lax.optimization_barrier((outgoing, up[1:], down[1:], planes[1:]))
    arrived = lax.all_to_all(outgoing, "grp", split_axis=0, concat_axis=0, tiled=True)
    merged = [piece] + [jnp.where(grp >= s, up[s], down[groups - s]) for s in range(1, groups)]
    entries_c = across_rows(merged, rows_n)
    panels = across_rows(planes, rows_n)

    wide = min(PIV, cols_here)
    needed = min(part, wide)
    zero = jnp.zeros((), f32)
    own_rows, added = [], []
    for at in range(rows_n):
        total, extra = zero, zero
        for s in range(groups):
            start = col * (cols_here // B)
            which = lax.dynamic_slice(quarters, ((grp - s) % groups, start), (1, wide // B))
            lanes_in = jnp.repeat(which == 0, B, axis=1)
            for t in range(rows_n):
                here = (row - t) % rows_n == at
                if at * part < wide:
                    total = total + jnp.where(here & (grp == s), entries_c[s * rows_n + t][:needed], 0.0)
                extra = extra + jnp.where(here & lanes_in, panels[s * rows_n + t][:, :wide], 0.0)
        if at * part < wide:
            own_rows.append(total)
        added.append(extra)
    own_rows = jnp.concatenate(own_rows, axis=0)[:wide]
    head = own_rows + jnp.pad(jnp.concatenate(added, axis=0).T, ((0, 0), (LEAD, 0)))
    heads = [head]
    for other in range(1, -(-PIV // cols_here)):
        wide = min(cols_here, PIV - other * cols_here)
        heads.append(lax.ppermute(head[:wide], "col", [(other, 0)]))
    head = bcast(jnp.concatenate(heads, axis=0) if len(heads) > 1 else head, "col", cols_n)

    mine = pl.pallas_call(
        mine_kernel,
        out_shape=shape((PIV, cols_here), f32),
        in_specs=[smem(), smem()] + [vmem()] * (len(entries_c) + len(panels)),
        out_specs=vmem(),
        scratch_shapes=[pltpu.VMEM((cols_here, PIV), f32), pltpu.VMEM((PIV - LEAD, cols_here), f32)],
        compiler_params=params(),
        cost_estimate=cost(6),
        name="mine",
    )(pos, quarters, *entries_c, *panels)
    y_n = cols_n // spans
    y_here = (col // spans - row) % y_n
    stride = y_n // 2
    while stride >= 1:
        pairs = []
        for r in range(rows_n):
            for y in range(0, y_n, 2 * stride):
                for k in range(spans):
                    source, target = (r + y) % y_n * spans + k, (r + y + stride) % y_n * spans + k
                    pairs.append((r * cols_n + source, r * cols_n + target))
        moved = lax.ppermute(mine, ("row", "col"), pairs)
        mine = jnp.where(y_here % (2 * stride) == stride, moved, mine)
        stride //= 2
    parts = [mine]
    for k in range(1, spans):
        pairs = [(y * spans + i, y * spans + (i + k) % spans) for y in range(y_n) for i in range(spans)]
        parts.append(lax.ppermute(mine, "col", pairs))
    inner = col % spans
    across = jnp.concatenate(
        [
            functools.reduce(lambda a, k: jnp.where((inner - s) % spans == k, parts[k], a), range(1, spans), parts[0])
            for s in range(spans)
        ],
        axis=1,
    )
    inverse = pl.pallas_call(
        head_kernel,
        out_shape=shape((PIV, PIV), f32),
        in_specs=[vmem()],
        out_specs=vmem(),
        scratch_shapes=[pltpu.VMEM((PIV, PIV), f32), pltpu.VMEM((PIV, PIV), f32), pltpu.VMEM((B, 2 * B), f32)],
        compiler_params=params(),
        cost_estimate=cost(25),
        name="head",
    )(head)

    lc3 = pl.pallas_call(
        columns_kernel,
        grid=(groups,),
        out_shape=shape((3 * PIV, groups * cols_here), bf16),
        in_specs=[smem(), smem(), vmem()] + [vmem()] * (len(entries_c) + len(panels)),
        out_specs=pl.BlockSpec((3 * PIV, cols_here), lambda u: (0, u)),
        scratch_shapes=[pltpu.VMEM((cols_here, PIV), f32), pltpu.VMEM((PIV - LEAD, cols_here), f32)],
        compiler_params=params(),
        cost_estimate=cost(23),
        name="columns",
    )(pos, quarters, inverse, *entries_c, *panels)

    tall = min(256, rows_here)
    lr, lr3 = pl.pallas_call(
        rows_kernel,
        grid=(rows_here // tall,),
        out_shape=(shape((rows_here, PIV), f32), shape((rows_here, 3 * PIV), bf16)),
        in_specs=[smem(), vmem(), pl.BlockSpec((PIV, tall), lambda i: (0, i))],
        out_specs=(pl.BlockSpec((tall, PIV), lambda i: (i, 0)), pl.BlockSpec((tall, 3 * PIV), lambda i: (i, 0))),
        compiler_params=params(),
        cost_estimate=cost(12),
        name="rows",
    )(pos, inverse, across)

    pair = 2
    tall = min(512, rows_here)
    result = pl.pallas_call(
        final_kernel,
        grid=(rows_here // tall, lanes // pair),
        out_shape=shape((rows_here, lanes * groups, B), f32),
        in_specs=[
            smem(),
            smem(),
            vmem(),
            pl.BlockSpec((tall, PIV), lambda i, p: (i, 0)),
            pl.BlockSpec((tall, 3 * PIV), lambda i, p: (i, 0)),
            vmem(),
            pl.BlockSpec((tall, pair * groups, B), lambda i, p: (i, p, 0)),
        ],
        out_specs=pl.BlockSpec((tall, pair * groups, B), lambda i, p: (i, p, 0)),
        scratch_shapes=[pltpu.VMEM((pair * groups, tall, B), f32), pltpu.SMEM((groups, row_blocks), jnp.int32)],
        compiler_params=params(),
        name="final",
    )(pos, quarters, arrived, lr, lr3, lc3, view)
    return result.reshape(rows_here, lanes, groups, B).transpose(0, 2, 1, 3).reshape(rows_here, groups, cols_here)


def solution(mesh):
    in_specs = (P("grp", "row", "col"), P(("grp", "row"), None, "col"), P(), P())
    out_specs = P(("grp", "row"), None, "col")
    return jax.shard_map(shards, mesh=mesh, in_specs=in_specs, out_specs=out_specs, check_vma=False)
```

```python
import functools

import jax
import jax.numpy as jnp
from jax import lax
from jax.experimental import pallas as pl
from jax.experimental.pallas import tpu as pltpu
from jax.sharding import PartitionSpec as P

B = 128
KC = 1
KP = 3
FC = 4096
LEAD = KC * B
PIV = KP * B
HIGHEST = lax.Precision.HIGHEST
VMEM_LIMIT = 60 * 1024 * 1024


def dot_nn(a, b, precision=HIGHEST):
    return lax.dot_general(a, b, (((1,), (0,)), ((), ())), precision=precision, preferred_element_type=jnp.float32)


def dot_nt(a, b, precision=HIGHEST):
    return lax.dot_general(a, b, (((1,), (1,)), ((), ())), precision=precision, preferred_element_type=jnp.float32)


def dot_bf(a, b):
    return lax.dot_general(a, b, (((1,), (0,)), ((), ())), preferred_element_type=jnp.float32)


def split(x):
    hi = x.astype(jnp.bfloat16)
    lo = (x - hi.astype(jnp.float32)).astype(jnp.bfloat16)
    return hi, lo


def vmem():
    return pl.BlockSpec(memory_space=pltpu.VMEM)


def smem():
    return pl.BlockSpec(memory_space=pltpu.SMEM)


def invert_factor(block, aug):
    n = block.shape[0]
    rows = lax.broadcasted_iota(jnp.int32, (n, n), 0)
    cols = lax.broadcasted_iota(jnp.int32, (n, n), 1)
    row_ids = lax.broadcasted_iota(jnp.int32, (n, 1), 0)
    lane_ids = lax.broadcasted_iota(jnp.int32, (1, n), 1)
    aug[:, :n] = block
    aug[:, n:] = jnp.where(rows == cols, 1.0, 0.0).astype(jnp.float32)

    many = 4

    def step(i, pivots):
        k = i * many
        rows_k = [aug[pl.ds(k + j, 1), :] for j in range(many)]
        body = aug[...]
        columns = [jnp.sum(jnp.where(cols == k + j, body[:, :n], 0.0), axis=1, keepdims=True) for j in range(many)]
        small = [
            [jnp.sum(jnp.where(lane_ids == k + b, rows_k[a][:, :n], 0.0), axis=1, keepdims=True) for b in range(many)]
            for a in range(many)
        ]
        factors = []
        for a in range(many):
            scale = 1.0 / small[a][a]
            for b in range(a + 1, many):
                ratio = small[a][b] * scale
                rows_k[b] = rows_k[b] - ratio * rows_k[a]
                columns[b] = columns[b] - columns[a] * ratio
                for c in range(b, many):
                    small[b][c] = small[b][c] - ratio * small[a][c]
            factors.append(jnp.where(row_ids >= k + many, columns[a] * scale, 0.0))
            pivots = jnp.where(row_ids == k + a, small[a][a], pivots)
        for a in range(many):
            body = body - factors[a] * rows_k[a]
        aug[...] = body
        for a in range(1, many):
            aug[pl.ds(k + a, 1), :] = rows_k[a]
        return pivots

    pivots = lax.fori_loop(0, n // many, step, jnp.ones((n, 1), jnp.float32))
    return aug[:, n:] / jnp.sqrt(pivots)


def extract_kernel(groups, view, *outs):
    for i, out in enumerate(outs):

        @pl.when(pl.program_id(0) == i)
        def _(out=out):
            for h in range(out.shape[1] // B):
                out[:, h * B : (h + 1) * B] = view[:, h * groups, :]


def child_kernel(pos, live, quarters, corner, strip, prow, lead, brow3, bcol3, panel, aug, below):
    rows_here, cols_here = strip.shape[0], prow.shape[1]
    share = lead.shape[0]
    grp, row, col = pos[0], pos[1], pos[2]
    live_end = live[grp] * B
    inverse = invert_factor(corner[:LEAD], aug)
    row_ids = row * rows_here + lax.broadcasted_iota(jnp.int32, (rows_here, 1), 0)
    col_ids = col * cols_here + lax.broadcasted_iota(jnp.int32, (1, cols_here), 1)
    live_rows = (row_ids >= LEAD) & (row_ids < live_end)
    live_cols = (col_ids >= LEAD) & (col_ids < live_end)
    bcol = jnp.where(live_cols, dot_nn(inverse, prow[...]), 0.0)
    below[...] = dot_nt(corner[LEAD:], inverse)
    tall = min(share, B)
    for i in range(0, share, tall):
        at = pl.multiple_of(row * share + i, tall)
        k = KC + lax.div(at, B)
        keep = live_cols & (k * B < live_end) & (quarters[grp, k] == 0)
        update = dot_nn(below[pl.ds(at, tall), :], bcol)
        value = jnp.where(keep, lead[i : i + tall, :] - update, 0.0)
        for g in range(panel.shape[0]):
            panel[g, i : i + tall, :] = value
    hi, lo = split(bcol)
    bcol3[:LEAD] = hi
    bcol3[LEAD : 2 * LEAD] = lo
    bcol3[2 * LEAD :] = hi
    hi, lo = split(jnp.where(live_rows, dot_nt(strip[...], inverse), 0.0))
    brow3[:, :LEAD] = hi
    brow3[:, LEAD : 2 * LEAD] = hi
    brow3[:, 2 * LEAD :] = lo


def outgoing_kernel(pos, live, quarters, front, brow3, bcol3, *refs):
    *outs, gathered, picked = refs
    rows_here, cols_here = front.shape
    row_blocks = rows_here // B
    slots = gathered.shape[0] // B
    grp, row, col = pos[0], pos[1], pos[2]
    live_end = live[grp] * B
    target = pl.program_id(0)

    def pick(b, count):
        hit = quarters[grp, row * row_blocks + b] == target

        @pl.when(hit & (count < slots))
        def _():
            picked[count] = b

        return count + hit.astype(jnp.int32)

    lax.fori_loop(0, row_blocks, pick, jnp.int32(0))
    for s in range(slots):
        at = pl.multiple_of(picked[s] * B, B)
        gathered[s * B : (s + 1) * B, :] = brow3[pl.ds(at, B), :]
    width = min(256, cols_here // len(outs))
    for n in range(cols_here // width):
        cut = slice(n * width, (n + 1) * width)
        product = dot_bf(gathered[...], bcol3[:, cut])
        col_ids = col * cols_here + n * width + lax.broadcasted_iota(jnp.int32, (1, width), 1)
        live_cols = (col_ids >= LEAD) & (col_ids < live_end)
        for s in range(slots):
            at = pl.multiple_of(picked[s] * B, B)
            first = row * rows_here + at
            keep = live_cols & (first >= LEAD) & (first < live_end)
            value = front[pl.ds(at, B), cut] - product[s * B : (s + 1) * B]
            which, inner = divmod(n * width, cols_here // len(outs))
            outs[which][0, s * B : (s + 1) * B, inner : inner + width] = jnp.where(keep, value, 0.0)


def head_kernel(head, inverse, work, factor, aug):
    work[...] = head[...]
    inverse[...] = jnp.zeros_like(inverse)
    for k in range(KP):
        kk = slice(k * B, (k + 1) * B)
        diag = invert_factor(work[kk, kk], aug)
        inverse[kk, kk] = diag
        for i in range(k + 1, KP):
            ii = slice(i * B, (i + 1) * B)
            factor[ii, kk] = dot_nt(work[ii, kk], diag)
        for i in range(k + 1, KP):
            for j in range(k + 1, i + 1):
                ii, jj = slice(i * B, (i + 1) * B), slice(j * B, (j + 1) * B)
                work[ii, jj] = work[ii, jj] - dot_nt(factor[ii, kk], factor[jj, kk])
        for j in range(k):
            jj = slice(j * B, (j + 1) * B)
            total = jnp.zeros((B, B), jnp.float32)
            for i in range(j, k):
                ii = slice(i * B, (i + 1) * B)
                total = total + dot_nn(factor[kk, ii], inverse[ii, jj])
            inverse[kk, jj] = -dot_nn(diag, total)


def place_pieces(pos, quarters, refs, quarter, entries, placed):
    groups = quarters.shape[0]
    own, own_panels, *others = refs
    pieces, panels = others[: len(others) // 2], others[len(others) // 2 :]
    rows_n = len(pieces) // groups + 1
    part, share = own.shape[1], own_panels.shape[1]
    col_blocks = placed.shape[1] // B
    row, col = pos[1], pos[2]
    placed[...] = jnp.zeros_like(placed)
    for s in range(groups):
        mine = [own.at[s]] + list(pieces[s * (rows_n - 1) : (s + 1) * (rows_n - 1)])
        added = [own_panels.at[s]] + list(panels[s * (rows_n - 1) : (s + 1) * (rows_n - 1)])

        @pl.when(quarter == s)
        def _(mine=mine):
            for t in range(rows_n):
                at = pl.multiple_of(lax.rem(row + rows_n - t, rows_n) * part, part)
                entries[pl.ds(at, part), :] = mine[t][...]

        for b in range(col_blocks):
            cut = slice(b * B, (b + 1) * B)

            @pl.when(quarters[s, col * col_blocks + b] == quarter)
            def _(added=added, cut=cut):
                for t in range(rows_n):
                    at = pl.multiple_of(lax.rem(row + rows_n - t, rows_n) * share, share)
                    placed[pl.ds(at, share), cut] += added[t][:, cut]


def columns_kernel(pos, quarters, inverse, *refs):
    lc3, entries, placed = refs[-3:]
    place_pieces(pos, quarters, refs[:-3], pl.program_id(0), entries, placed)
    value = dot_nt(inverse[...], entries[...]) + dot_nn(inverse[:, LEAD:], placed[...])
    hi, lo = split(value)
    lc3[:PIV] = hi
    lc3[PIV : 2 * PIV] = lo
    lc3[2 * PIV :] = hi


def mine_kernel(pos, quarters, *refs):
    mine, entries, placed = refs[-3:]
    place_pieces(pos, quarters, refs[:-3], pos[0], entries, placed)
    for k in range(KP):
        kk = slice(k * B, (k + 1) * B)
        value = jnp.transpose(entries[:, kk])
        mine[kk] = value if k < KC else value + placed[(k - KC) * B : (k - KC + 1) * B]


def rows_kernel(pos, inverse, across, lr, lr3):
    height = lr.shape[0]
    value = jnp.transpose(dot_nn(inverse[...], across[...]))
    first = pos[3] + pl.program_id(0) * height
    row_ids = first + lax.broadcasted_iota(jnp.int32, (height, PIV), 0)
    inside = lax.broadcasted_iota(jnp.int32, (height, PIV), 1)
    value = jnp.where(inside <= row_ids, value, 0.0)
    lr[...] = value
    hi, lo = split(value)
    lr3[:, :PIV] = hi
    lr3[:, PIV : 2 * PIV] = hi
    lr3[:, 2 * PIV :] = lo


def final_kernel(offset, pos, quarters, arrived, lr, lr3, lc3, entries, *refs):
    out, acc, slot_of = refs[-3:]
    groups = quarters.shape[0]
    cols_here = lc3.shape[1] // groups
    height = entries.shape[0]
    pair = entries.shape[1] // groups
    width = pair * B
    row_blocks = slot_of.shape[1]
    blocks = height // B
    grp, row, col, first_row = pos[0], pos[1], pos[2], pos[3]
    rb, p = pl.program_id(0), pl.program_id(1)

    @pl.when((rb == 0) & (p == 0))
    def _():
        for g in range(groups):

            def note(b, count, g=g):
                hit = quarters[g, row * row_blocks + b] == grp
                slot_of[g, b] = jnp.where(hit, count, -1)
                return count + hit.astype(jnp.int32)

            lax.fori_loop(0, row_blocks, note, jnp.int32(0))

    inner = pl.multiple_of(p * width, width)
    start = pl.multiple_of((p + offset) * width, width)
    left = lr3[...]
    for u in range(groups):
        product = dot_bf(left, lc3[:, pl.ds(pl.multiple_of(u * cols_here + start, width), width)])
        for h in range(pair):
            acc[h * groups + u] = -product[:, h * B : (h + 1) * B]

    for g in range(groups):
        for b in range(blocks):
            slot = slot_of[g, rb * blocks + b]

            @pl.when(slot >= 0)
            def _(g=g, b=b, slot=slot):
                at = pl.multiple_of(slot * B, B)
                for h in range(pair):
                    place = quarters[g, col * (cols_here // B) + (p + offset) * pair + h]
                    value = arrived[g, pl.ds(at, B), pl.ds(pl.multiple_of(inner + h * B, B), B)]
                    acc[h * groups + place, b * B : (b + 1) * B, :] += value

    step = 32
    first = first_row + rb * height

    def plain(i, carry):
        at = pl.multiple_of(i * step, step)
        value = jnp.swapaxes(acc[:, pl.ds(at, step), :], 0, 1)
        out[pl.ds(at, step)] = entries[pl.ds(at, step)] + value
        return carry

    begin_col = col * cols_here + start
    special = (first < PIV) | (begin_col < PIV)

    @pl.when(jnp.logical_not(special))
    def _():
        lax.fori_loop(0, height // step, plain, 0)

    @pl.when(special)
    def _():
        row_ids = first + lax.broadcasted_iota(jnp.int32, (height, 1), 0)
        for h in range(pair):
            for u in range(groups):
                here = begin_col + h * B
                is_pivot = (here < PIV) if u == 0 else False
                if u == 0:
                    strip = lr[:, pl.ds(pl.multiple_of(jnp.where(is_pivot, here, 0), B), B)]
                    other = jnp.where(row_ids < PIV, 0.0, acc[h * groups])
                    acc[h * groups] = jnp.where(is_pivot, strip, other)
                else:
                    acc[h * groups + u] = jnp.where(row_ids < PIV, 0.0, acc[h * groups + u])

        def masked(i, carry):
            at = pl.multiple_of(i * step, step)
            value = jnp.swapaxes(acc[:, pl.ds(at, step), :], 0, 1)
            shape = (step, pair * groups, B)
            ids = first + at + lax.broadcasted_iota(jnp.int32, shape, 0)
            which = lax.broadcasted_iota(jnp.int32, shape, 1)
            pivot_col = (which % groups == 0) & (begin_col + (which // groups) * B < PIV)
            keep = (ids >= PIV) & jnp.logical_not(pivot_col)
            out[pl.ds(at, step)] = jnp.where(keep, entries[pl.ds(at, step)], 0.0) + value
            return carry

        lax.fori_loop(0, height // step, masked, 0)


def params(**kw):
    return pltpu.CompilerParams(vmem_limit_bytes=VMEM_LIMIT, **kw)


def cost(us):
    return pl.CostEstimate(flops=10**6, bytes_accessed=us * 3_500_000, transcendentals=0)


def bcast(value, axis, size):
    here = lax.axis_index(axis)
    stride = size // 2
    while stride >= 1:
        pairs = [(i, i + stride) for i in range(0, size, 2 * stride)]
        moved = lax.ppermute(value, axis, pairs)
        value = jnp.where(here % (2 * stride) == stride, moved, value)
        stride //= 2
    return value


def ring_shift(value, axis, size, by):
    return lax.ppermute(value, axis, [(i, (i + by) % size) for i in range(size)])


def planes_of(value, groups):
    return lax.all_to_all(jnp.broadcast_to(value[None], (groups,) + value.shape), "grp", split_axis=0, concat_axis=0)


def across_rows(planes, rows_n):
    groups = planes.shape[0]
    return [ring_shift(planes[g], "row", rows_n, t) for g in range(groups) for t in range(1, rows_n)]


def shards(child_fronts, parent_entries, child_live, quarters):
    front = child_fronts[0]
    rows_here, cols_here = front.shape
    groups, rows_n, cols_n = (lax.axis_size(a) for a in ("grp", "row", "col"))
    grp, row, col = (lax.axis_index(a) for a in ("grp", "row", "col"))
    row_blocks = rows_here // B
    slots = row_blocks // groups
    spans = rows_here // cols_here
    first_row = (grp * rows_n + row) * rows_here
    ids = jnp.arange(8, dtype=jnp.int32)
    pos = jnp.where(ids == 0, grp, jnp.where(ids == 1, row, jnp.where(ids == 2, col, first_row)))
    pos = pos.astype(jnp.int32)
    f32, bf16 = jnp.float32, jnp.bfloat16
    shape = jax.ShapeDtypeStruct

    lanes = cols_here // B
    view = parent_entries.reshape(rows_here, groups, lanes, B).transpose(0, 2, 1, 3).reshape(rows_here, lanes * groups, B)
    wide = min(PIV, cols_here)
    part = cols_here // rows_n
    deep = -(-wide // B * groups // 8) * 8
    own = pl.pallas_call(
        functools.partial(extract_kernel, groups),
        grid=(spans * rows_n,),
        out_shape=[shape((part, wide), f32)] * (spans * rows_n),
        in_specs=[pl.BlockSpec((part, deep, B), lambda i: (i, 0, 0))],
        out_specs=[vmem()] * (spans * rows_n),
        compiler_params=params(),
        cost_estimate=cost(6),
        name="extract",
    )(view)
    if wide < PIV:
        owners = range(1, -(-PIV // cols_here))
        widths = [min(cols_here, PIV - o * cols_here) for o in owners]
        moved = [[lax.ppermute(x[:, :w], "col", [(o, 0)]) for o, w in zip(owners, widths)] for x in own]
        own = [jnp.concatenate([x] + more, axis=1) for x, more in zip(own, moved)]
    pieces = []
    for h in range(spans):
        for r in range(rows_n):
            pairs = [(s * cols_n, r * cols_n + s * spans + h) for s in range(rows_n)]
            pieces.append(lax.ppermute(own[h * rows_n + r], ("row", "col"), pairs))
    pieces, front = lax.optimization_barrier((pieces, front))
    piece = functools.reduce(lambda a, b: a + b, pieces)
    entry_planes = planes_of(piece, groups)

    share = (PIV - LEAD) // rows_n
    lead = jnp.where(row == 0, front[LEAD : LEAD + share], 0.0)
    for r in range(1, rows_n):
        at = LEAD + r * share
        lead = lead + lax.ppermute(front[at : at + share], "row", [(0, r)])
    strip = bcast(front[:, :LEAD], "col", cols_n)
    prow = bcast(front[:LEAD], "row", rows_n)
    corner = bcast(bcast(front[:PIV, :LEAD], "col", cols_n), "row", rows_n)
    brow3, bcol3, panel = pl.pallas_call(
        child_kernel,
        out_shape=(
            shape((rows_here, 3 * LEAD), bf16),
            shape((3 * LEAD, cols_here), bf16),
            shape((groups, share, cols_here), f32),
        ),
        in_specs=[smem(), smem(), smem(), vmem(), vmem(), vmem(), vmem()],
        out_specs=(vmem(), vmem(), vmem()),
        scratch_shapes=[pltpu.VMEM((LEAD, 2 * LEAD), f32), pltpu.VMEM((PIV - LEAD, LEAD), f32)],
        compiler_params=params(),
        cost_estimate=cost(15),
        name="child",
    )(pos, child_live, quarters, corner, strip, prow, lead)

    pair = lanes
    chunks = 1
    outgoing = pl.pallas_call(
        outgoing_kernel,
        grid=(groups,),
        out_shape=[shape((groups, slots * B, cols_here // chunks), f32)] * chunks,
        in_specs=[smem(), smem(), smem(), vmem(), vmem(), vmem()],
        out_specs=[pl.BlockSpec((1, slots * B, cols_here // chunks), lambda d: (d, 0, 0))] * chunks,
        scratch_shapes=[pltpu.VMEM((slots * B, 3 * LEAD), bf16), pltpu.SMEM((slots,), jnp.int32)],
        compiler_params=params(),
        cost_estimate=cost(10),
        name="outgoing",
    )(pos, child_live, quarters, front, brow3, bcol3)

    entry_planes, panel = lax.optimization_barrier((entry_planes, panel))
    planes = lax.all_to_all(panel, "grp", split_axis=0, concat_axis=0, tiled=True)
    entries_c = across_rows(entry_planes, rows_n)
    early = entries_c[: len(entries_c) // 2]
    outgoing, planes, early = lax.optimization_barrier((outgoing, planes, early))
    entries_c[: len(early)] = early
    arrived = [lax.all_to_all(x, "grp", split_axis=0, concat_axis=0, tiled=True) for x in outgoing]
    panels = across_rows(planes, rows_n)

    sources = [entry_planes, planes] + entries_c + panels

    wide = min(PIV, cols_here)
    needed = min(part, wide)
    zero = jnp.zeros((), f32)
    own_rows, added = [], []
    for at in range(rows_n):
        total, extra = zero, zero
        for s in range(groups):
            start = col * (cols_here // B)
            which = lax.dynamic_slice(quarters, (s, start), (1, wide // B))
            lanes_in = jnp.repeat(which == 0, B, axis=1)
            for t in range(rows_n):
                here = (row - t) % rows_n == at
                if at * part < wide and s == 0:
                    value = entries_c[t - 1] if t else entry_planes[0]
                    total = total + jnp.where(here, value[:needed], 0.0)
                value = panels[s * (rows_n - 1) + t - 1] if t else planes[s]
                extra = extra + jnp.where(here & lanes_in, value[:, :wide], 0.0)
        if at * part < wide:
            own_rows.append(total)
        added.append(extra)
    own_rows = jnp.concatenate(own_rows, axis=0)[:wide]
    head = own_rows + jnp.pad(jnp.concatenate(added, axis=0).T, ((0, 0), (LEAD, 0)))
    heads = [head]
    for other in range(1, -(-PIV // cols_here)):
        wide = min(cols_here, PIV - other * cols_here)
        heads.append(lax.ppermute(head[:wide], "col", [(other, 0)]))
    head = bcast(jnp.concatenate(heads, axis=0) if len(heads) > 1 else head, "col", cols_n)

    mine = pl.pallas_call(
        mine_kernel,
        out_shape=shape((PIV, cols_here), f32),
        in_specs=[smem(), smem()] + [vmem()] * len(sources),
        out_specs=vmem(),
        scratch_shapes=[pltpu.VMEM((cols_here, PIV), f32), pltpu.VMEM((PIV - LEAD, cols_here), f32)],
        compiler_params=params(),
        cost_estimate=cost(6),
        name="mine",
    )(pos, quarters, *sources)
    mine, head = lax.optimization_barrier((mine, head))
    inverse = pl.pallas_call(
        head_kernel,
        out_shape=shape((PIV, PIV), f32),
        in_specs=[vmem()],
        out_specs=vmem(),
        scratch_shapes=[pltpu.VMEM((PIV, PIV), f32), pltpu.VMEM((PIV, PIV), f32), pltpu.VMEM((B, 2 * B), f32)],
        compiler_params=params(),
        cost_estimate=cost(25),
        name="head",
    )(head)

    y_n = cols_n // spans
    y_here = (col // spans - row) % y_n
    stride = y_n // 2
    while stride >= 1:
        pairs = []
        for r in range(rows_n):
            for y in range(0, y_n, 2 * stride):
                for k in range(spans):
                    source, target = (r + y) % y_n * spans + k, (r + y + stride) % y_n * spans + k
                    pairs.append((r * cols_n + source, r * cols_n + target))
        moved = lax.ppermute(mine, ("row", "col"), pairs)
        if stride == 1:
            moved, inverse = lax.optimization_barrier((moved, inverse))
        mine = jnp.where(y_here % (2 * stride) == stride, moved, mine)
        stride //= 2
    parts = [mine]
    for k in range(1, spans):
        pairs = [(y * spans + i, y * spans + (i + k) % spans) for y in range(y_n) for i in range(spans)]
        parts.append(lax.ppermute(mine, "col", pairs))
    inner = col % spans
    across = jnp.concatenate(
        [
            functools.reduce(lambda a, k: jnp.where((inner - s) % spans == k, parts[k], a), range(1, spans), parts[0])
            for s in range(spans)
        ],
        axis=1,
    )
    lc3 = pl.pallas_call(
        columns_kernel,
        grid=(groups,),
        out_shape=shape((3 * PIV, groups * cols_here), bf16),
        in_specs=[smem(), smem(), vmem()] + [vmem()] * len(sources),
        out_specs=pl.BlockSpec((3 * PIV, cols_here), lambda u: (0, u)),
        scratch_shapes=[pltpu.VMEM((cols_here, PIV), f32), pltpu.VMEM((PIV - LEAD, cols_here), f32)],
        compiler_params=params(),
        cost_estimate=cost(23),
        name="columns",
    )(pos, quarters, inverse, *sources)

    tall = min(256, rows_here)
    lr, lr3 = pl.pallas_call(
        rows_kernel,
        grid=(rows_here // tall,),
        out_shape=(shape((rows_here, PIV), f32), shape((rows_here, 3 * PIV), bf16)),
        in_specs=[smem(), vmem(), pl.BlockSpec((PIV, tall), lambda i: (0, i))],
        out_specs=(pl.BlockSpec((tall, PIV), lambda i: (i, 0)), pl.BlockSpec((tall, 3 * PIV), lambda i: (i, 0))),
        compiler_params=params(),
        cost_estimate=cost(12),
        name="rows",
    )(pos, inverse, across)

    tall = min(256, rows_here)
    steps = lanes // pair // chunks
    result = None
    for n in range(chunks):
        block = pl.BlockSpec((tall, pair * groups, B), lambda i, p, n=n: (i, p + n * steps, 0))
        before = [] if result is None else [result]
        result = pl.pallas_call(
            functools.partial(final_kernel, n * steps),
            grid=(rows_here // tall, steps),
            out_shape=shape((rows_here, lanes * groups, B), f32),
            in_specs=[
                smem(),
                smem(),
                vmem(),
                pl.BlockSpec((tall, PIV), lambda i, p: (i, 0)),
                pl.BlockSpec((tall, 3 * PIV), lambda i, p: (i, 0)),
                vmem(),
                block,
            ]
            + [pl.BlockSpec(memory_space=pl.ANY)] * len(before),
            out_specs=block,
            scratch_shapes=[pltpu.VMEM((pair * groups, tall, B), f32), pltpu.SMEM((groups, row_blocks), jnp.int32)],
            input_output_aliases={7: 0} if before else {},
            compiler_params=params(),
            cost_estimate=cost(50 // chunks),
            name="final",
        )(pos, quarters, arrived[n], lr, lr3, lc3, view, *before)
    return result.reshape(rows_here, lanes, groups, B).transpose(0, 2, 1, 3).reshape(rows_here, groups, cols_here)


def solution(mesh):
    in_specs = (P("grp", "row", "col"), P(("grp", "row"), None, "col"), P(), P())
    out_specs = P(("grp", "row"), None, "col")
    return jax.shard_map(shards, mesh=mesh, in_specs=in_specs, out_specs=out_specs, check_vma=False)
```

```python
import functools

import jax
import jax.numpy as jnp
from jax import lax
from jax.experimental import pallas as pl
from jax.experimental.pallas import tpu as pltpu
from jax.sharding import PartitionSpec as P

B = 128
KC = 1
KP = 3
FC = 4096
LEAD = KC * B
PIV = KP * B
HIGHEST = lax.Precision.HIGHEST
VMEM_LIMIT = 60 * 1024 * 1024


def dot_nn(a, b, precision=HIGHEST):
    return lax.dot_general(a, b, (((1,), (0,)), ((), ())), precision=precision, preferred_element_type=jnp.float32)


def dot_nt(a, b, precision=HIGHEST):
    return lax.dot_general(a, b, (((1,), (1,)), ((), ())), precision=precision, preferred_element_type=jnp.float32)


def dot_bf(a, b):
    return lax.dot_general(a, b, (((1,), (0,)), ((), ())), preferred_element_type=jnp.float32)


def split(x):
    hi = x.astype(jnp.bfloat16)
    lo = (x - hi.astype(jnp.float32)).astype(jnp.bfloat16)
    return hi, lo


def vmem():
    return pl.BlockSpec(memory_space=pltpu.VMEM)


def smem():
    return pl.BlockSpec(memory_space=pltpu.SMEM)


def invert_factor(block, aug):
    n = block.shape[0]
    rows = lax.broadcasted_iota(jnp.int32, (n, n), 0)
    cols = lax.broadcasted_iota(jnp.int32, (n, n), 1)
    row_ids = lax.broadcasted_iota(jnp.int32, (n, 1), 0)
    lane_ids = lax.broadcasted_iota(jnp.int32, (1, n), 1)
    aug[:, :n] = block
    aug[:, n:] = jnp.where(rows == cols, 1.0, 0.0).astype(jnp.float32)

    many = 4

    def step(i, pivots):
        k = i * many
        rows_k = [aug[pl.ds(k + j, 1), :] for j in range(many)]
        body = aug[...]
        columns = [jnp.sum(jnp.where(cols == k + j, body[:, :n], 0.0), axis=1, keepdims=True) for j in range(many)]
        small = [
            [jnp.sum(jnp.where(lane_ids == k + b, rows_k[a][:, :n], 0.0), axis=1, keepdims=True) for b in range(many)]
            for a in range(many)
        ]
        factors = []
        for a in range(many):
            scale = 1.0 / small[a][a]
            for b in range(a + 1, many):
                ratio = small[a][b] * scale
                rows_k[b] = rows_k[b] - ratio * rows_k[a]
                columns[b] = columns[b] - columns[a] * ratio
                for c in range(b, many):
                    small[b][c] = small[b][c] - ratio * small[a][c]
            factors.append(jnp.where(row_ids >= k + many, columns[a] * scale, 0.0))
            pivots = jnp.where(row_ids == k + a, small[a][a], pivots)
        for a in range(many):
            body = body - factors[a] * rows_k[a]
        aug[...] = body
        for a in range(1, many):
            aug[pl.ds(k + a, 1), :] = rows_k[a]
        return pivots

    pivots = lax.fori_loop(0, n // many, step, jnp.ones((n, 1), jnp.float32))
    return aug[:, n:] / jnp.sqrt(pivots)


def extract_kernel(groups, view, *outs):
    for i, out in enumerate(outs):

        @pl.when(pl.program_id(0) == i)
        def _(out=out):
            for h in range(out.shape[1] // B):
                out[:, h * B : (h + 1) * B] = view[:, h * groups, :]


def child_kernel(pos, live, quarters, corner, strip, prow, lead, brow3, bcol3, panel, aug, below):
    rows_here, cols_here = strip.shape[0], prow.shape[1]
    share = lead.shape[0]
    grp, row, col = pos[0], pos[1], pos[2]
    live_end = live[grp] * B
    inverse = invert_factor(corner[:LEAD], aug)
    row_ids = row * rows_here + lax.broadcasted_iota(jnp.int32, (rows_here, 1), 0)
    col_ids = col * cols_here + lax.broadcasted_iota(jnp.int32, (1, cols_here), 1)
    live_rows = (row_ids >= LEAD) & (row_ids < live_end)
    live_cols = (col_ids >= LEAD) & (col_ids < live_end)
    bcol = jnp.where(live_cols, dot_nn(inverse, prow[...]), 0.0)
    below[...] = dot_nt(corner[LEAD:], inverse)
    tall = min(share, B)
    for i in range(0, share, tall):
        at = pl.multiple_of(row * share + i, tall)
        k = KC + lax.div(at, B)
        keep = live_cols & (k * B < live_end) & (quarters[grp, k] == 0)
        update = dot_nn(below[pl.ds(at, tall), :], bcol)
        value = jnp.where(keep, lead[i : i + tall, :] - update, 0.0)
        for g in range(panel.shape[0]):
            panel[g, i : i + tall, :] = value
    hi, lo = split(bcol)
    bcol3[:LEAD] = hi
    bcol3[LEAD : 2 * LEAD] = lo
    bcol3[2 * LEAD :] = hi
    hi, lo = split(jnp.where(live_rows, dot_nt(strip[...], inverse), 0.0))
    brow3[:, :LEAD] = hi
    brow3[:, LEAD : 2 * LEAD] = hi
    brow3[:, 2 * LEAD :] = lo


def outgoing_kernel(pos, live, quarters, front, brow3, bcol3, *refs):
    *outs, gathered, picked = refs
    rows_here, cols_here = front.shape
    row_blocks = rows_here // B
    slots = gathered.shape[0] // B
    grp, row, col = pos[0], pos[1], pos[2]
    live_end = live[grp] * B
    target = pl.program_id(0)

    def pick(b, count):
        hit = quarters[grp, row * row_blocks + b] == target

        @pl.when(hit & (count < slots))
        def _():
            picked[count] = b

        return count + hit.astype(jnp.int32)

    lax.fori_loop(0, row_blocks, pick, jnp.int32(0))
    for s in range(slots):
        at = pl.multiple_of(picked[s] * B, B)
        gathered[s * B : (s + 1) * B, :] = brow3[pl.ds(at, B), :]
    width = min(256, cols_here // len(outs))
    for n in range(cols_here // width):
        cut = slice(n * width, (n + 1) * width)
        product = dot_bf(gathered[...], bcol3[:, cut])
        col_ids = col * cols_here + n * width + lax.broadcasted_iota(jnp.int32, (1, width), 1)
        live_cols = (col_ids >= LEAD) & (col_ids < live_end)
        for s in range(slots):
            at = pl.multiple_of(picked[s] * B, B)
            first = row * rows_here + at
            keep = live_cols & (first >= LEAD) & (first < live_end)
            value = front[pl.ds(at, B), cut] - product[s * B : (s + 1) * B]
            which, inner = divmod(n * width, cols_here // len(outs))
            outs[which][0, s * B : (s + 1) * B, inner : inner + width] = jnp.where(keep, value, 0.0)


def head_kernel(head, inverse, work, factor, aug):
    work[...] = head[...]
    inverse[...] = jnp.zeros_like(inverse)
    for k in range(KP):
        kk = slice(k * B, (k + 1) * B)
        diag = invert_factor(work[kk, kk], aug)
        inverse[kk, kk] = diag
        for i in range(k + 1, KP):
            ii = slice(i * B, (i + 1) * B)
            factor[ii, kk] = dot_nt(work[ii, kk], diag)
        for i in range(k + 1, KP):
            for j in range(k + 1, i + 1):
                ii, jj = slice(i * B, (i + 1) * B), slice(j * B, (j + 1) * B)
                work[ii, jj] = work[ii, jj] - dot_nt(factor[ii, kk], factor[jj, kk])
        for j in range(k):
            jj = slice(j * B, (j + 1) * B)
            total = jnp.zeros((B, B), jnp.float32)
            for i in range(j, k):
                ii = slice(i * B, (i + 1) * B)
                total = total + dot_nn(factor[kk, ii], inverse[ii, jj])
            inverse[kk, jj] = -dot_nn(diag, total)


def place_pieces(pos, quarters, refs, quarter, entries, placed):
    groups = quarters.shape[0]
    own, own_panels, *others = refs
    pieces, panels = others[: len(others) // 2], others[len(others) // 2 :]
    rows_n = len(pieces) // groups + 1
    part, share = own.shape[1], own_panels.shape[1]
    col_blocks = placed.shape[1] // B
    row, col = pos[1], pos[2]
    placed[...] = jnp.zeros_like(placed)
    for s in range(groups):
        mine = [own.at[s]] + list(pieces[s * (rows_n - 1) : (s + 1) * (rows_n - 1)])
        added = [own_panels.at[s]] + list(panels[s * (rows_n - 1) : (s + 1) * (rows_n - 1)])

        @pl.when(quarter == s)
        def _(mine=mine):
            for t in range(rows_n):
                at = pl.multiple_of(lax.rem(row + rows_n - t, rows_n) * part, part)
                entries[pl.ds(at, part), :] = mine[t][...]

        for b in range(col_blocks):
            cut = slice(b * B, (b + 1) * B)

            @pl.when(quarters[s, col * col_blocks + b] == quarter)
            def _(added=added, cut=cut):
                for t in range(rows_n):
                    at = pl.multiple_of(lax.rem(row + rows_n - t, rows_n) * share, share)
                    placed[pl.ds(at, share), cut] += added[t][:, cut]


def columns_kernel(pos, quarters, inverse, *refs):
    lc3, entries, placed = refs[-3:]
    place_pieces(pos, quarters, refs[:-3], pl.program_id(0), entries, placed)
    entries[:, LEAD:] += jnp.transpose(placed[...])
    value = dot_nt(inverse[...], entries[...])
    hi, lo = split(value)
    lc3[:PIV] = hi
    lc3[PIV : 2 * PIV] = lo
    lc3[2 * PIV :] = hi


def mine_kernel(pos, quarters, *refs):
    mine, entries, placed = refs[-3:]
    place_pieces(pos, quarters, refs[:-3], pos[0], entries, placed)
    for k in range(KP):
        kk = slice(k * B, (k + 1) * B)
        value = jnp.transpose(entries[:, kk])
        mine[kk] = value if k < KC else value + placed[(k - KC) * B : (k - KC + 1) * B]


def rows_kernel(pos, inverse, across, lr, lr3):
    height = lr.shape[0]
    value = jnp.transpose(dot_nn(inverse[...], across[...]))
    first = pos[3] + pl.program_id(0) * height
    row_ids = first + lax.broadcasted_iota(jnp.int32, (height, PIV), 0)
    inside = lax.broadcasted_iota(jnp.int32, (height, PIV), 1)
    value = jnp.where(inside <= row_ids, value, 0.0)
    lr[...] = value
    hi, lo = split(value)
    lr3[:, :PIV] = hi
    lr3[:, PIV : 2 * PIV] = hi
    lr3[:, 2 * PIV :] = lo


def final_kernel(offset, pos, quarters, incoming, lr, lr3, lc3, entries, *refs):
    out, acc, slot_of, arrived, ready = refs[-5:]
    groups = quarters.shape[0]
    cols_here = lc3.shape[1] // groups
    height = entries.shape[0]
    pair = entries.shape[1] // groups
    width = pair * B
    row_blocks = slot_of.shape[1]
    blocks = height // B
    grp, row, col, first_row = pos[0], pos[1], pos[2], pos[3]
    rb, p = pl.program_id(0), pl.program_id(1)

    load = pltpu.make_async_copy(incoming, arrived, ready)

    @pl.when((rb == 0) & (p == 0))
    def _():
        load.start()
        for g in range(groups):

            def note(b, count, g=g):
                hit = quarters[g, row * row_blocks + b] == grp
                slot_of[g, b] = jnp.where(hit, count, -1)
                return count + hit.astype(jnp.int32)

            lax.fori_loop(0, row_blocks, note, jnp.int32(0))

    inner = pl.multiple_of(p * width, width)
    start = pl.multiple_of((p + offset) * width, width)
    left = lr3[...]
    for u in range(groups):
        product = dot_bf(left, lc3[:, pl.ds(pl.multiple_of(u * cols_here + start, width), width)])
        for h in range(pair):
            acc[h * groups + u] = -product[:, h * B : (h + 1) * B]

    @pl.when((rb == 0) & (p == 0))
    def _():
        load.wait()

    for g in range(groups):
        for b in range(blocks):
            slot = slot_of[g, rb * blocks + b]

            @pl.when(slot >= 0)
            def _(g=g, b=b, slot=slot):
                at = pl.multiple_of(slot * B, B)
                for h in range(pair):
                    place = quarters[g, col * (cols_here // B) + (p + offset) * pair + h]
                    value = arrived[g, pl.ds(at, B), pl.ds(pl.multiple_of(inner + h * B, B), B)]
                    acc[h * groups + place, b * B : (b + 1) * B, :] += value

    step = 32
    first = first_row + rb * height

    def plain(i, carry):
        at = pl.multiple_of(i * step, step)
        value = jnp.swapaxes(acc[:, pl.ds(at, step), :], 0, 1)
        out[pl.ds(at, step)] = entries[pl.ds(at, step)] + value
        return carry

    begin_col = col * cols_here + start
    special = (first < PIV) | (begin_col < PIV)

    @pl.when(jnp.logical_not(special))
    def _():
        lax.fori_loop(0, height // step, plain, 0)

    @pl.when(special)
    def _():
        row_ids = first + lax.broadcasted_iota(jnp.int32, (height, 1), 0)
        for h in range(pair):
            for u in range(groups):
                here = begin_col + h * B
                is_pivot = (here < PIV) if u == 0 else False
                if u == 0:
                    strip = lr[:, pl.ds(pl.multiple_of(jnp.where(is_pivot, here, 0), B), B)]
                    other = jnp.where(row_ids < PIV, 0.0, acc[h * groups])
                    acc[h * groups] = jnp.where(is_pivot, strip, other)
                else:
                    acc[h * groups + u] = jnp.where(row_ids < PIV, 0.0, acc[h * groups + u])

        def masked(i, carry):
            at = pl.multiple_of(i * step, step)
            value = jnp.swapaxes(acc[:, pl.ds(at, step), :], 0, 1)
            shape = (step, pair * groups, B)
            ids = first + at + lax.broadcasted_iota(jnp.int32, shape, 0)
            which = lax.broadcasted_iota(jnp.int32, shape, 1)
            pivot_col = (which % groups == 0) & (begin_col + (which // groups) * B < PIV)
            keep = (ids >= PIV) & jnp.logical_not(pivot_col)
            out[pl.ds(at, step)] = jnp.where(keep, entries[pl.ds(at, step)], 0.0) + value
            return carry

        lax.fori_loop(0, height // step, masked, 0)


def params(**kw):
    return pltpu.CompilerParams(vmem_limit_bytes=VMEM_LIMIT, **kw)


def cost(us):
    return pl.CostEstimate(flops=10**6, bytes_accessed=us * 3_500_000, transcendentals=0)


def bcast(value, axis, size):
    here = lax.axis_index(axis)
    stride = size // 2
    while stride >= 1:
        pairs = [(i, i + stride) for i in range(0, size, 2 * stride)]
        moved = lax.ppermute(value, axis, pairs)
        value = jnp.where(here % (2 * stride) == stride, moved, value)
        stride //= 2
    return value


def ring_shift(value, axis, size, by):
    return lax.ppermute(value, axis, [(i, (i + by) % size) for i in range(size)])


def planes_of(value, groups):
    return lax.all_to_all(jnp.broadcast_to(value[None], (groups,) + value.shape), "grp", split_axis=0, concat_axis=0)


def across_rows(planes, rows_n):
    groups = planes.shape[0]
    return [ring_shift(planes[g], "row", rows_n, t) for g in range(groups) for t in range(1, rows_n)]


def shards(child_fronts, parent_entries, child_live, quarters):
    front = child_fronts[0]
    rows_here, cols_here = front.shape
    groups, rows_n, cols_n = (lax.axis_size(a) for a in ("grp", "row", "col"))
    grp, row, col = (lax.axis_index(a) for a in ("grp", "row", "col"))
    row_blocks = rows_here // B
    slots = row_blocks // groups
    spans = rows_here // cols_here
    first_row = (grp * rows_n + row) * rows_here
    ids = jnp.arange(8, dtype=jnp.int32)
    pos = jnp.where(ids == 0, grp, jnp.where(ids == 1, row, jnp.where(ids == 2, col, first_row)))
    pos = pos.astype(jnp.int32)
    f32, bf16 = jnp.float32, jnp.bfloat16
    shape = jax.ShapeDtypeStruct

    lanes = cols_here // B
    view = parent_entries.reshape(rows_here, groups, lanes, B).transpose(0, 2, 1, 3).reshape(rows_here, lanes * groups, B)
    wide = min(PIV, cols_here)
    part = cols_here // rows_n
    deep = -(-wide // B * groups // 8) * 8
    own = []
    each = spans * rows_n // 2 or 1
    for start in range(0, spans * rows_n, each):
        own += pl.pallas_call(
            functools.partial(extract_kernel, groups),
            grid=(each,),
            out_shape=[shape((part, wide), f32)] * each,
            in_specs=[pl.BlockSpec((part, deep, B), lambda i, start=start: (i + start, 0, 0))],
            out_specs=[vmem()] * each,
            compiler_params=params(),
            cost_estimate=cost(4),
            name="extract",
        )(view)
    if wide < PIV:
        owners = range(1, -(-PIV // cols_here))
        widths = [min(cols_here, PIV - o * cols_here) for o in owners]
        moved = [[lax.ppermute(x[:, :w], "col", [(o, 0)]) for o, w in zip(owners, widths)] for x in own]
        own = [jnp.concatenate([x] + more, axis=1) for x, more in zip(own, moved)]
    pieces = []
    for h in range(spans):
        for r in range(rows_n):
            pairs = [(s * cols_n, r * cols_n + s * spans + h) for s in range(rows_n)]
            pieces.append(lax.ppermute(own[h * rows_n + r], ("row", "col"), pairs))
    pieces, front = lax.optimization_barrier((pieces, front))
    piece = functools.reduce(lambda a, b: a + b, pieces)
    entry_planes = planes_of(piece, groups)

    share = (PIV - LEAD) // rows_n
    lead = jnp.where(row == 0, front[LEAD : LEAD + share], 0.0)
    for r in range(1, rows_n):
        at = LEAD + r * share
        lead = lead + lax.ppermute(front[at : at + share], "row", [(0, r)])
    strip = bcast(front[:, :LEAD], "col", cols_n)
    prow = bcast(front[:LEAD], "row", rows_n)
    corner = bcast(bcast(front[:PIV, :LEAD], "col", cols_n), "row", rows_n)
    brow3, bcol3, panel = pl.pallas_call(
        child_kernel,
        out_shape=(
            shape((rows_here, 3 * LEAD), bf16),
            shape((3 * LEAD, cols_here), bf16),
            shape((groups, share, cols_here), f32),
        ),
        in_specs=[smem(), smem(), smem(), vmem(), vmem(), vmem(), vmem()],
        out_specs=(vmem(), vmem(), vmem()),
        scratch_shapes=[pltpu.VMEM((LEAD, 2 * LEAD), f32), pltpu.VMEM((PIV - LEAD, LEAD), f32)],
        compiler_params=params(),
        cost_estimate=cost(15),
        name="child",
    )(pos, child_live, quarters, corner, strip, prow, lead)

    pair = lanes
    chunks = 1
    outgoing = pl.pallas_call(
        outgoing_kernel,
        grid=(groups,),
        out_shape=[shape((groups, slots * B, cols_here // chunks), f32)] * chunks,
        in_specs=[smem(), smem(), smem(), vmem(), vmem(), vmem()],
        out_specs=[pl.BlockSpec((1, slots * B, cols_here // chunks), lambda d: (d, 0, 0))] * chunks,
        scratch_shapes=[pltpu.VMEM((slots * B, 3 * LEAD), bf16), pltpu.SMEM((slots,), jnp.int32)],
        compiler_params=params(),
        cost_estimate=cost(10),
        name="outgoing",
    )(pos, child_live, quarters, front, brow3, bcol3)

    entry_planes, panel = lax.optimization_barrier((entry_planes, panel))
    planes = lax.all_to_all(panel, "grp", split_axis=0, concat_axis=0, tiled=True)
    entries_c = across_rows(entry_planes, rows_n)
    early = entries_c[: len(entries_c) // 2]
    outgoing, planes, early = lax.optimization_barrier((outgoing, planes, early))
    entries_c[: len(early)] = early
    arrived = [lax.all_to_all(x, "grp", split_axis=0, concat_axis=0, tiled=True) for x in outgoing]
    panels = across_rows(planes, rows_n)

    sources = [entry_planes, planes] + entries_c + panels

    wide = min(PIV, cols_here)
    needed = min(part, wide)
    zero = jnp.zeros((), f32)
    own_rows, added = [], []
    for at in range(rows_n):
        total, extra = zero, zero
        for s in range(groups):
            start = col * (cols_here // B)
            which = lax.dynamic_slice(quarters, (s, start), (1, wide // B))
            lanes_in = jnp.repeat(which == 0, B, axis=1)
            for t in range(rows_n):
                here = (row - t) % rows_n == at
                if at * part < wide and s == 0:
                    value = entries_c[t - 1] if t else entry_planes[0]
                    total = total + jnp.where(here, value[:needed], 0.0)
                value = panels[s * (rows_n - 1) + t - 1] if t else planes[s]
                extra = extra + jnp.where(here & lanes_in, value[:, :wide], 0.0)
        if at * part < wide:
            own_rows.append(total)
        added.append(extra)
    own_rows = jnp.concatenate(own_rows, axis=0)[:wide]
    head = own_rows + jnp.pad(jnp.concatenate(added, axis=0).T, ((0, 0), (LEAD, 0)))
    heads = [head]
    for other in range(1, -(-PIV // cols_here)):
        wide = min(cols_here, PIV - other * cols_here)
        heads.append(lax.ppermute(head[:wide], "col", [(other, 0)]))
    head = bcast(jnp.concatenate(heads, axis=0) if len(heads) > 1 else head, "col", cols_n)

    mine = pl.pallas_call(
        mine_kernel,
        out_shape=shape((PIV, cols_here), f32),
        in_specs=[smem(), smem()] + [vmem()] * len(sources),
        out_specs=vmem(),
        scratch_shapes=[pltpu.VMEM((cols_here, PIV), f32), pltpu.VMEM((PIV - LEAD, cols_here), f32)],
        compiler_params=params(),
        cost_estimate=cost(6),
        name="mine",
    )(pos, quarters, *sources)
    mine, head = lax.optimization_barrier((mine, head))
    inverse = pl.pallas_call(
        head_kernel,
        out_shape=shape((PIV, PIV), f32),
        in_specs=[vmem()],
        out_specs=vmem(),
        scratch_shapes=[pltpu.VMEM((PIV, PIV), f32), pltpu.VMEM((PIV, PIV), f32), pltpu.VMEM((B, 2 * B), f32)],
        compiler_params=params(),
        cost_estimate=cost(25),
        name="head",
    )(head)

    y_n = cols_n // spans
    y_here = (col // spans - row) % y_n
    stride = y_n // 2
    while stride >= 1:
        pairs = []
        for r in range(rows_n):
            for y in range(0, y_n, 2 * stride):
                for k in range(spans):
                    source, target = (r + y) % y_n * spans + k, (r + y + stride) % y_n * spans + k
                    pairs.append((r * cols_n + source, r * cols_n + target))
        moved = lax.ppermute(mine, ("row", "col"), pairs)
        if stride == 1:
            moved, inverse = lax.optimization_barrier((moved, inverse))
        mine = jnp.where(y_here % (2 * stride) == stride, moved, mine)
        stride //= 2
    parts = [mine]
    for k in range(1, spans):
        pairs = [(y * spans + i, y * spans + (i + k) % spans) for y in range(y_n) for i in range(spans)]
        parts.append(lax.ppermute(mine, "col", pairs))
    inner = col % spans
    across = jnp.concatenate(
        [
            functools.reduce(lambda a, k: jnp.where((inner - s) % spans == k, parts[k], a), range(1, spans), parts[0])
            for s in range(spans)
        ],
        axis=1,
    )
    lc3 = pl.pallas_call(
        columns_kernel,
        grid=(groups,),
        out_shape=shape((3 * PIV, groups * cols_here), bf16),
        in_specs=[smem(), smem(), vmem()] + [vmem()] * len(sources),
        out_specs=pl.BlockSpec((3 * PIV, cols_here), lambda u: (0, u)),
        scratch_shapes=[pltpu.VMEM((cols_here, PIV), f32), pltpu.VMEM((PIV - LEAD, cols_here), f32)],
        compiler_params=params(),
        cost_estimate=cost(23),
        name="columns",
    )(pos, quarters, inverse, *sources)

    tall = min(256, rows_here)
    lr, lr3 = pl.pallas_call(
        rows_kernel,
        grid=(rows_here // tall,),
        out_shape=(shape((rows_here, PIV), f32), shape((rows_here, 3 * PIV), bf16)),
        in_specs=[smem(), vmem(), pl.BlockSpec((PIV, tall), lambda i: (0, i))],
        out_specs=(pl.BlockSpec((tall, PIV), lambda i: (i, 0)), pl.BlockSpec((tall, 3 * PIV), lambda i: (i, 0))),
        compiler_params=params(),
        cost_estimate=cost(12),
        name="rows",
    )(pos, inverse, across)

    tall = min(256, rows_here)
    steps = lanes // pair // chunks
    result = None
    for n in range(chunks):
        block = pl.BlockSpec((tall, pair * groups, B), lambda i, p, n=n: (i, p + n * steps, 0))
        before = [] if result is None else [result]
        result = pl.pallas_call(
            functools.partial(final_kernel, n * steps),
            grid=(rows_here // tall, steps),
            out_shape=shape((rows_here, lanes * groups, B), f32),
            in_specs=[
                smem(),
                smem(),
                pl.BlockSpec(memory_space=pl.ANY),
                pl.BlockSpec((tall, PIV), lambda i, p: (i, 0)),
                pl.BlockSpec((tall, 3 * PIV), lambda i, p: (i, 0)),
                vmem(),
                block,
            ]
            + [pl.BlockSpec(memory_space=pl.ANY)] * len(before),
            out_specs=block,
            scratch_shapes=[
                pltpu.VMEM((pair * groups, tall, B), f32),
                pltpu.SMEM((groups, row_blocks), jnp.int32),
                pltpu.VMEM(arrived[n].shape, f32),
                pltpu.SemaphoreType.DMA(()),
            ],
            input_output_aliases={7: 0} if before else {},
            compiler_params=params(),
            cost_estimate=cost(50 // chunks),
            name="final",
        )(pos, quarters, arrived[n], lr, lr3, lc3, view, *before)
    return result.reshape(rows_here, lanes, groups, B).transpose(0, 2, 1, 3).reshape(rows_here, groups, cols_here)


def solution(mesh):
    in_specs = (P("grp", "row", "col"), P(("grp", "row"), None, "col"), P(), P())
    out_specs = P(("grp", "row"), None, "col")
    return jax.shard_map(shards, mesh=mesh, in_specs=in_specs, out_specs=out_specs, check_vma=False)
```
